256 devices in a mesh: segment: 2 (over core), angle: 16 (over x_lo, z), tile: 8 (over y, x_hi).
Axes of the slice: x: 4 (x_hi: 2, x_lo: 2; x = x_hi * 2 + x_lo), y: 4, z: 8, core: 2. Of those that a mesh axis runs over, the one named last changes fastest.
Arguments:
- sinogram: float32 [64, 32, 4096], P(('segment', 'angle'), 'tile'), may hold values from -6 to 6
- paganin_width: float32 [1], replicated, may hold values from 2 to 8
- window_block: int32 [64, 8], replicated, may hold values from 0 to 28
Outputs:
- volume: float32 [8, 32, 65536], P('tile', None, ('segment', 'angle'))
The draws below stay inside these ranges and needn't reach their ends.
All inputs are finite; a program needn't handle non-finite values.
Results may differ from the reference program's by a relative error of at most 0.0035.
Values may be sent and summed in bfloat16 or wider, within the bound.
A program may use at most 64 MiB of HBM per device.

```python
import math
import jax
import jax.numpy as jnp
from jax import lax

W = 4096
WIN = 512
BAND = 128
SLICES = 32
TCOLS = 256
ANGLES = 64
TROWS = 256
TILES = 8


def touch_ends(drawn, stream_key, smallest, top_value):
    longest = drawn.shape.index(max(drawn.shape))
    spots = []
    for shift in (0, 1):
        where = [jax.random.randint(jax.random.fold_in(stream_key, axis), (), 0, length) for axis, length in enumerate(drawn.shape)]
        where[longest] = (where[longest] + shift) % drawn.shape[longest]
        spots.append(tuple(where))
    return drawn.at[spots[0]].set(smallest).at[spots[1]].set(top_value)


def block_scale(stream_key, shape, shards, low, largest):
    loudness = 1.0
    for dim, parts in shards:
        steps = jax.random.uniform(jax.random.fold_in(jax.random.fold_in(stream_key, 6), dim), (parts,), jnp.float32, low / len(shards), largest / len(shards))
        loudness = loudness * jnp.repeat(jnp.exp(steps), shape[dim] // parts).reshape((-1,) + (1,) * (len(shape) - 1 - dim))
    return loudness


def normal_values(own_key, shape, deviation, most, shards=(), held_as=jnp.bfloat16):
    loudness = block_scale(own_key, shape, shards, -0.22, 0.18) if shards else 1.0
    drawn = jax.random.normal(own_key, shape, jnp.float32) * deviation * loudness
    return jnp.minimum(jnp.maximum(drawn, -most), most).astype(held_as)


def setup_inputs(seed: int = 0) -> dict:
    key_list = jax.random.split(jax.random.key(seed), 4)
    return {
        "sinogram": normal_values(key_list[0], (ANGLES, SLICES, W), 1.0, 6.0, ((0, 32), (1, 8)), jnp.float32),
        "paganin_width": jnp.clip(jnp.exp(jax.random.uniform(key_list[1], (1,), jnp.float32, math.log(2.0), math.log(8.0))), 2.0, 8.0),
        "window_block": touch_ends(jax.random.randint(key_list[2], (ANGLES, TILES), 0, (W - WIN) // 128 + 1), jax.random.fold_in(key_list[2], 1), 0, ((W - WIN) // 128 + 1) - 1).astype(jnp.int32),
    }


def band_kernels(width):
    inner = jnp.arange(128, dtype=jnp.int32)
    offsets = (jnp.arange(3, dtype=jnp.int32) - 1)[:, None, None] * 128 + inner[None, :, None] - inner[None, None, :]
    spread = offsets.astype(jnp.float32)
    inside = jnp.abs(offsets) <= BAND
    taps = jnp.arange(-BAND, BAND + 1).astype(jnp.float32)
    normal_total = jnp.sum(jnp.exp(-jnp.abs(taps) / width))
    paganin = jnp.where(inside, jnp.exp(-jnp.abs(spread) / width) / normal_total, 0.0)
    squared = jnp.maximum(spread * spread, 1.0)
    odd_taps = jnp.where(inside & (offsets % 2 == 1), -1.0 / (math.pi * math.pi * squared), 0.0)
    ramp = jnp.where(offsets == 0, 0.25, odd_taps)
    return paganin, ramp


def apply_band(rows, kernels):
    row_count, bins = rows.shape
    blocks = bins // 128
    shaped = rows.reshape(row_count, blocks, 128)
    padded = jnp.pad(shaped, ((0, 0), (1, 1), (0, 0)))
    result = jnp.zeros_like(shaped)
    for offset in range(3):
        result = result + jnp.einsum("rbi,io->rbo", padded[:, offset:offset + blocks], kernels[offset], precision=lax.Precision.HIGHEST)
    return result.reshape(row_count, bins)


def hat_block(angles, angle_total, row_first, row_count, tile_rows):
    theta = math.pi * angles.astype(jnp.float32) / angle_total
    rows_here = (row_first + jnp.arange(row_count, dtype=jnp.int32)).astype(jnp.float32) - (tile_rows - 1) / 2.0
    columns = jnp.arange(TCOLS).astype(jnp.float32) - (TCOLS - 1) / 2.0
    across = columns[None, None, :] * jnp.cos(theta)[:, None, None] + rows_here[None, :, None] * jnp.sin(theta)[:, None, None]
    across = across.reshape(angles.shape[0], row_count * TCOLS) + WIN / 2.0
    detector = jnp.arange(WIN).astype(jnp.float32)
    weight = jnp.maximum(0.0, 1.0 - jnp.abs(across[:, None, :] - detector[None, :, None]))
    return weight.astype(jnp.bfloat16)


def reference(sinogram, paganin_width, window_block):
    smoothing, ramping = band_kernels(paganin_width[0])
    rows = sinogram.reshape(ANGLES * SLICES, W)
    filtered = apply_band(apply_band(rows, smoothing), ramping).astype(jnp.bfloat16).reshape(ANGLES, SLICES, W)

    def one_tile(tile_index):
        def advance(total, angle):
            start = (window_block[angle, tile_index] * 128).astype(jnp.int32)
            window = lax.dynamic_slice_in_dim(filtered[angle], start, WIN, 1)
            weights = hat_block(angle[None], ANGLES, 0, TROWS, TROWS)[0]
            return total + jnp.dot(window, weights, preferred_element_type=jnp.float32), None

        start_total = jnp.zeros((SLICES, TROWS * TCOLS), jnp.float32)
        total, ignored = lax.scan(advance, start_total, jnp.arange(ANGLES, dtype=jnp.int32))
        return total

    return lax.map(one_tile, jnp.arange(TILES, dtype=jnp.int32))
```

```python
import functools
import math

import jax
import jax.numpy as jnp
import numpy as np
from jax import lax
from jax.experimental import pallas as pl
from jax.experimental.pallas import tpu as pltpu
from jax.sharding import PartitionSpec as P

MESH = pl.DeviceIdType.MESH
LANES = 128
BAND = 128
ROWS_DEV = 8
TCOLS = 256
ANGLES = 64
TROWS = 256
TILES = 8
ZS = 8
XS = 2
BLOCKS = 32
KEEP = 3
BINS_SHIFT = 64
CENTRE = 256 - BINS_SHIFT

F32 = jnp.float32
BF16 = jnp.bfloat16

GATHER = lax.GatherDimensionNumbers(
    offset_dims=(),
    collapsed_slice_dims=(1,),
    start_index_map=(1,),
    operand_batching_dims=(0,),
    start_indices_batching_dims=(0,),
)


def lane_gather(values, index):
    return lax.gather(
        values, index[:, :, None], GATHER, (1, 1), mode=lax.GatherScatterMode.PROMISE_IN_BOUNDS
    )


def iota(shape, axis):
    return lax.broadcasted_iota(jnp.int32, shape, axis)


def split(value):
    high = value.astype(BF16)
    return high, (value - high.astype(F32)).astype(BF16)


def dot3(left, right):
    left_high, left_low = split(left)
    right_high, right_low = split(right)
    return (
        jnp.dot(left_high, right_high, preferred_element_type=F32)
        + jnp.dot(left_low, right_high, preferred_element_type=F32)
        + jnp.dot(left_high, right_low, preferred_element_type=F32)
    )


def smoothing_band(width):
    shape = (3 * LANES, LANES)
    offset = iota(shape, 0) - LANES - iota(shape, 1)
    spread = jnp.abs(offset).astype(F32)
    taps = jnp.exp(-(iota((1, LANES), 1) + 1).astype(F32) / width)
    total = 1.0 + 2.0 * jnp.sum(taps)
    return jnp.where(jnp.abs(offset) <= BAND, jnp.exp(-spread / width) / total, 0.0)


def ramp_band():
    shape = (4 * LANES, LANES)
    offset = iota(shape, 0) - LANES - BINS_SHIFT - iota(shape, 1)
    size = jnp.abs(offset)
    spread = size.astype(F32)
    odd = jnp.where(
        (size <= BAND) & (size % 2 == 1),
        -1.0 / (math.pi * math.pi * jnp.maximum(spread * spread, 1.0)),
        0.0,
    )
    return jnp.where(offset == 0, 0.25, odd)


def filter_rows(sino_ref, width_ref, padded, smooth, filtered):
    zero = jnp.zeros((8, LANES), F32)
    padded[0:8] = zero
    padded[264:272] = zero
    smooth[0:8] = zero
    smooth[264:272] = zero
    for block in range(BLOCKS):
        columns = slice(block * LANES, (block + 1) * LANES)
        padded[(block + 1) * 8 : (block + 2) * 8] = jnp.concatenate(
            [sino_ref[0, :, columns], sino_ref[1, :, columns]], axis=0
        )
    left = jnp.concatenate([padded[8 * k : 8 * k + 256] for k in range(3)], axis=1)
    width = jnp.full((1, 1), width_ref[0], F32)
    smooth[8:264] = dot3(left, smoothing_band(width))
    left = jnp.concatenate([smooth[8 * k : 8 * k + 248] for k in range(4)], axis=1)
    filtered[...] = dot3(left, ramp_band()).reshape(BLOCKS - 1, 8, LANES)


def kernel(
    sino_ref,
    width_ref,
    window_ref,
    cos_ref,
    sin_ref,
    out_ref,
    padded,
    smooth,
    filtered,
    outgoing,
    held,
    total,
    partner_part,
    arrived_part,
    plane_send,
    plane_recv,
    ring_send,
    ring_recv,
    local_sem,
    part_send,
    part_recv,
):
    core = lax.axis_index("segment")
    chip = lax.axis_index("angle")
    tile = lax.axis_index("tile")
    x_low = chip // ZS
    z = chip % ZS
    spot = x_low * TILES + tile
    up = (z + 1) % ZS
    down = (z + ZS - 1) % ZS

    def plane_device(step):
        other = (spot + step) % (XS * TILES)
        return (core, (other // TILES) * ZS + z, other % TILES)

    neighbours = {0: (core, x_low * ZS + up, tile), 1: (core, x_low * ZS + down, tile)}
    partner = (1 - core, chip, tile)

    barrier = pltpu.get_barrier_semaphore()
    for step in range(1, XS * TILES):
        pl.semaphore_signal(barrier, inc=1, device_id=plane_device(step), device_id_type=MESH)
    for way in (0, 1):
        pl.semaphore_signal(barrier, inc=1, device_id=neighbours[way], device_id_type=MESH)
    pl.semaphore_signal(barrier, inc=1, device_id=partner, device_id_type=MESH)

    filter_rows(sino_ref, width_ref, padded, smooth, filtered)

    lower = iota((8, LANES), 0) < 4
    first_angle = (core * XS * ZS + chip) * 2
    for other in range(TILES):
        first = window_ref[first_angle, other]
        second = window_ref[first_angle + 1, other]
        for block in range(KEEP):
            outgoing[other, block] = jnp.where(
                lower, filtered[first + block], filtered[second + block]
            ).astype(BF16)

    @pl.loop(0, 32)
    def _(unit):
        total[unit] = jnp.zeros((64, LANES), F32)

    pl.semaphore_wait(barrier, XS * TILES + 2)

    own = pltpu.make_async_copy(outgoing.at[tile], held.at[z, x_low, tile], local_sem)
    own.start()
    sends = []
    for step in range(1, XS * TILES):
        copy = pltpu.make_async_remote_copy(
            src_ref=outgoing.at[(spot + step) % TILES],
            dst_ref=held.at[z, x_low, tile],
            send_sem=plane_send.at[step],
            recv_sem=plane_recv.at[step],
            device_id=plane_device(step),
            device_id_type=MESH,
        )
        copy.start()
        sends.append(copy)

    def ring_copy(way, hop, part):
        source = (z + ZS - hop) % ZS if way == 0 else (z + hop) % ZS
        return pltpu.make_async_remote_copy(
            src_ref=held.at[source, part],
            dst_ref=held.at[source, part],
            send_sem=ring_send.at[way, hop, part],
            recv_sem=ring_recv.at[way, hop, part],
            device_id=neighbours[way],
            device_id_type=MESH,
        )

    lane = iota((8, LANES), 1)
    lane_f = lane.astype(F32)
    lane16 = iota((16, LANES), 1).astype(jnp.int16)
    last_lane = lane == LANES - 1
    own_row = ((core * XS * ZS + chip) * ROWS_DEV).astype(F32) - (TROWS - 1) / 2.0
    partner_row = (((1 - core) * XS * ZS + chip) * ROWS_DEV).astype(F32) - (TROWS - 1) / 2.0

    def compute(source, part):
        angle = (core * XS * ZS + part * ZS + source) * 2
        cosine = jnp.where(lower, cos_ref[angle], cos_ref[angle + 1])
        sine = jnp.where(lower, sin_ref[angle], sin_ref[angle + 1])
        values, slopes = [], []
        for pair in range(TILES // 2):
            value_row, slope_row = [], []
            here = [
                [held[source, part, 2 * pair + half, block].astype(F32) for block in range(KEEP)]
                for half in (0, 1)
            ]
            moved = [[pltpu.roll(v, LANES - 1, 1) for v in row] for row in here]
            for block in range(KEEP):
                diffs = []
                for half in (0, 1):
                    after = moved[half][min(block + 1, KEEP - 1)]
                    diffs.append(
                        jnp.where(last_lane, after, moved[half][block]) - here[half][block]
                    )
                value_row.append(
                    jnp.concatenate([here[0][block], here[1][block]], axis=0).astype(BF16)
                )
                slope_row.append(jnp.concatenate(diffs, axis=0).astype(BF16))
            values.append(value_row)
            slopes.append(slope_row)
        spans, starts = [], []
        for half in (0, 1):
            left_end = half * LANES - (TCOLS - 1) / 2.0
            spans.append((lane_f + left_end) * cosine + float(CENTRE))
            end = jnp.where(cosine >= 0.0, left_end, left_end + LANES - 1.0)
            starts.append(end * cosine + float(CENTRE))
        for row in range(2 * ROWS_DEV):
            y = (partner_row if row < ROWS_DEV else own_row) + float(row % ROWS_DEV)
            lift = sine * y
            for half in (0, 1):
                unit = row * 2 + half
                u = spans[half] + lift
                k = u.astype(jnp.int32)
                part_way = u - k.astype(F32)
                k = k & (LANES - 1)
                index = jnp.concatenate([k, k], axis=0).astype(jnp.int16)
                begin = (starts[half] + lift).astype(jnp.int32)
                begin = jnp.concatenate([begin, begin], axis=0).astype(jnp.int16)
                past0 = begin > lane16
                past1 = begin > lane16 + jnp.int16(LANES)
                for pair in range(TILES // 2):
                    v = values[pair]
                    d = slopes[pair]
                    v = jnp.where(past1, v[2], jnp.where(past0, v[1], v[0]))
                    d = jnp.where(past1, d[2], jnp.where(past0, d[1], d[0]))
                    v = lane_gather(v, index).astype(F32)
                    d = lane_gather(d, index).astype(F32)
                    for half_row in (0, 1):
                        rows = slice(half_row * 8, half_row * 8 + 8)
                        at = slice(pair * 16 + half_row * 8, pair * 16 + half_row * 8 + 8)
                        total[unit, at] += v[rows] + part_way * d[rows]

    own.wait()
    for step in range(1, XS * TILES):
        sends[step - 1].wait_recv()
    for part in range(XS):
        for way in (0, 1):
            ring_copy(way, 0, part).start()

    @pl.loop(0, XS)
    def _(part):
        compute(z, part)

    @pl.loop(1, 4)
    def _(hop):
        @pl.loop(0, XS)
        def _(part):
            for way in (0, 1):
                ring_copy(way, hop - 1, part).wait_recv()

                @pl.when((hop < 3) | (part == way))
                def _():
                    ring_copy(way, hop, part).start()

            @pl.loop(0, 2)
            def _(way):
                compute(jnp.where(way == 0, (z + ZS - hop) % ZS, (z + hop) % ZS), part)

    ring_copy(0, 3, 0).wait_recv()
    ring_copy(1, 3, 1).wait_recv()

    @pl.loop(0, XS)
    def _(part):
        compute((z + 4) % ZS, part)

    def fold(unit):
        result = []
        for group in range(4):
            pieces = []
            for half in (0, 1):
                v = total[unit, group * 16 + half * 8 : group * 16 + half * 8 + 8]
                pieces.append(v + pltpu.roll(v, 4, 0))
            result.append(jnp.where(lower, pieces[0], pieces[1]))
        return jnp.concatenate(result, axis=0)

    for unit in range(16):
        partner_part[unit] = fold(unit)
    swaps = []
    swap = pltpu.make_async_remote_copy(
        src_ref=partner_part,
        dst_ref=arrived_part,
        send_sem=part_send,
        recv_sem=part_recv,
        device_id=partner,
        device_id_type=MESH,
    )
    swap.start()
    for unit in range(16):
        out_ref[0, :, unit * LANES : (unit + 1) * LANES] = fold(unit + 16)
    swap.wait_recv()
    for unit in range(16):
        out_ref[0, :, unit * LANES : (unit + 1) * LANES] += arrived_part[unit]

    swap.wait_send()
    for copy in sends:
        copy.wait_send()
    for hop in range(4):
        for part in range(XS):
            for way in (0, 1):
                if hop < 3 or part == way:
                    ring_copy(way, hop, part).wait_send()


def body(sinogram, paganin_width, window_block):
    angles = np.pi * np.arange(ANGLES) / ANGLES
    cosines = jnp.asarray(np.cos(angles).astype(np.float32))
    sines = jnp.asarray(np.sin(angles).astype(np.float32))
    smem = pl.BlockSpec(memory_space=pltpu.SMEM)
    vmem = pl.BlockSpec(memory_space=pltpu.VMEM)
    return pl.pallas_call(
        kernel,
        out_shape=jax.ShapeDtypeStruct((1, 32, ROWS_DEV * TCOLS), F32),
        in_specs=[vmem, smem, smem, smem, smem],
        out_specs=vmem,
        scratch_shapes=[
            pltpu.VMEM((272, LANES), F32),
            pltpu.VMEM((272, LANES), F32),
            pltpu.VMEM((BLOCKS - 1, 8, LANES), F32),
            pltpu.VMEM((TILES, KEEP, 8, LANES), BF16),
            pltpu.VMEM((ZS, XS, TILES, KEEP, 8, LANES), BF16),
            pltpu.VMEM((32, 64, LANES), F32),
            pltpu.VMEM((16, 32, LANES), F32),
            pltpu.VMEM((16, 32, LANES), F32),
            pltpu.SemaphoreType.DMA((XS * TILES,)),
            pltpu.SemaphoreType.DMA((XS * TILES,)),
            pltpu.SemaphoreType.DMA((2, 4, XS)),
            pltpu.SemaphoreType.DMA((2, 4, XS)),
            pltpu.SemaphoreType.DMA,
            pltpu.SemaphoreType.DMA,
            pltpu.SemaphoreType.DMA,
        ],
        compiler_params=pltpu.CompilerParams(collective_id=0, has_side_effects=True),
    )(sinogram, paganin_width, window_block, cosines, sines)


def solution(mesh):
    in_specs = (P(("segment", "angle"), "tile", None), P(), P())
    out_specs = P("tile", None, ("segment", "angle"))
    return jax.shard_map(body, mesh=mesh, in_specs=in_specs, out_specs=out_specs, check_vma=False)
```

```python
import functools
import math

import jax
import jax.numpy as jnp
import numpy as np
from jax import lax
from jax.experimental import pallas as pl
from jax.experimental.pallas import tpu as pltpu
from jax.sharding import PartitionSpec as P

MESH = pl.DeviceIdType.MESH
LANES = 128
BAND = 128
ROWS_DEV = 8
TCOLS = 256
ANGLES = 64
TROWS = 256
TILES = 8
ZS = 8
XS = 2
BLOCKS = 32
KEEP = 3
BINS_SHIFT = 64
CENTRE = 256 - BINS_SHIFT
LAG = 3


def ring_distance(step):
    return sum(min(part, 4 - part) for part in step)


PLANE_STEPS = sorted(
    ((a, b) for a in range(4) for b in range(4) if a or b), key=ring_distance, reverse=True
)

F32 = jnp.float32
BF16 = jnp.bfloat16

GATHER = lax.GatherDimensionNumbers(
    offset_dims=(),
    collapsed_slice_dims=(1,),
    start_index_map=(1,),
    operand_batching_dims=(0,),
    start_indices_batching_dims=(0,),
)


def lane_gather(values, index):
    return lax.gather(
        values, index[:, :, None], GATHER, (1, 1), mode=lax.GatherScatterMode.PROMISE_IN_BOUNDS
    )


def iota(shape, axis):
    return lax.broadcasted_iota(jnp.int32, shape, axis)


def split(value):
    high = value.astype(BF16)
    return high, (value - high.astype(F32)).astype(BF16)


def dot3(left, right):
    left_high, left_low = split(left)
    right_high, right_low = split(right)
    return (
        jnp.dot(left_high, right_high, preferred_element_type=F32)
        + jnp.dot(left_low, right_high, preferred_element_type=F32)
        + jnp.dot(left_high, right_low, preferred_element_type=F32)
    )


def smoothing_band(width):
    shape = (3 * LANES, LANES)
    offset = iota(shape, 0) - LANES - iota(shape, 1)
    spread = jnp.abs(offset).astype(F32)
    taps = jnp.exp(-(iota((1, LANES), 1) + 1).astype(F32) / width)
    total = 1.0 + 2.0 * jnp.sum(taps)
    return jnp.where(jnp.abs(offset) <= BAND, jnp.exp(-spread / width) / total, 0.0)


def ramp_band():
    shape = (4 * LANES, LANES)
    offset = iota(shape, 0) - LANES - BINS_SHIFT - iota(shape, 1)
    size = jnp.abs(offset)
    spread = size.astype(F32)
    odd = jnp.where(
        (size <= BAND) & (size % 2 == 1),
        -1.0 / (math.pi * math.pi * jnp.maximum(spread * spread, 1.0)),
        0.0,
    )
    return jnp.where(offset == 0, 0.25, odd)


def filter_rows(sino_ref, width_ref, padded, smooth, filtered):
    zero = jnp.zeros((8, LANES), F32)
    padded[0:8] = zero
    padded[264:272] = zero
    smooth[0:8] = zero
    smooth[264:272] = zero
    for block in range(BLOCKS):
        columns = slice(block * LANES, (block + 1) * LANES)
        padded[(block + 1) * 8 : (block + 2) * 8] = jnp.concatenate(
            [sino_ref[0, :, columns], sino_ref[1, :, columns]], axis=0
        )
    left = jnp.concatenate([padded[8 * k : 8 * k + 256] for k in range(3)], axis=1)
    width = jnp.full((1, 1), width_ref[0], F32)
    smooth[8:264] = dot3(left, smoothing_band(width))
    left = jnp.concatenate([smooth[8 * k : 8 * k + 248] for k in range(4)], axis=1)
    filtered[...] = dot3(left, ramp_band()).reshape(BLOCKS - 1, 8, LANES)


def kernel(
    sino_ref,
    width_ref,
    window_ref,
    cos_ref,
    sin_ref,
    out_ref,
    padded,
    smooth,
    filtered,
    column,
    held,
    total,
    partner_part,
    arrived_part,
    column_send,
    column_recv,
    plane_send,
    plane_recv,
    local_sem,
    part_send,
    part_recv,
):
    core = lax.axis_index("segment")
    chip = lax.axis_index("angle")
    tile = lax.axis_index("tile")
    z = chip % ZS
    spot = (chip // ZS) * TILES + tile
    x = (tile % 2) * 2 + chip // ZS
    y = tile // 2

    def plane_peer(step):
        other_x = (x + step[0]) % 4
        other_y = (y + step[1]) % 4
        other_tile = other_y * 2 + other_x // 2
        return other_tile, (core, (other_x % 2) * ZS + z, other_tile)

    def column_peer(shift):
        return (core, chip - z + (z + shift) % ZS, tile)

    partner = (1 - core, chip, tile)

    barrier = pltpu.get_barrier_semaphore()
    for step in PLANE_STEPS:
        pl.semaphore_signal(barrier, inc=1, device_id=plane_peer(step)[1], device_id_type=MESH)
    for shift in range(1, ZS):
        pl.semaphore_signal(barrier, inc=1, device_id=column_peer(shift), device_id_type=MESH)
    pl.semaphore_signal(barrier, inc=1, device_id=partner, device_id_type=MESH)

    filter_rows(sino_ref, width_ref, padded, smooth, filtered)

    lower = iota((8, LANES), 0) < 4
    first_angle = (core * XS * ZS + chip) * 2
    for other in range(TILES):
        first = window_ref[other, first_angle]
        second = window_ref[other, first_angle + 1]
        for block in range(KEEP):
            column[z, other, block] = jnp.where(
                lower, filtered[first + block], filtered[second + block]
            ).astype(BF16)

    @pl.loop(0, 32)
    def _(unit):
        total[unit] = jnp.zeros((64, LANES), F32)

    pl.semaphore_wait(barrier, len(PLANE_STEPS) + ZS)

    def column_shift(turn):
        far = (ZS + 1 - turn) // 2
        return jnp.where(turn == 0, 0, jnp.where(turn % 2 == 0, far, ZS - far))

    def column_copy(turn):
        return pltpu.make_async_remote_copy(
            src_ref=column.at[z],
            dst_ref=column.at[z],
            send_sem=column_send.at[turn],
            recv_sem=column_recv.at[turn],
            device_id=column_peer(column_shift(turn)),
            device_id_type=MESH,
        )

    for turn in range(1, ZS):
        column_copy(turn).start()

    def slot(turn):
        return (z + ZS - column_shift(turn)) % ZS

    def own_copy(turn):
        return pltpu.make_async_copy(
            column.at[slot(turn), tile], held.at[slot(turn), spot], local_sem.at[turn]
        )

    def spread(turn):
        source = slot(turn)
        own_copy(turn).start()
        for step in PLANE_STEPS:
            other_tile, device = plane_peer(step)
            pltpu.make_async_remote_copy(
                src_ref=column.at[source, other_tile],
                dst_ref=held.at[source, spot],
                send_sem=plane_send.at[turn],
                recv_sem=plane_recv.at[turn],
                device_id=device,
                device_id_type=MESH,
            ).start()

    def all_of_plane(turn, sem):
        some = held.at[slot(turn), pl.ds(0, len(PLANE_STEPS))]
        return pltpu.make_async_copy(some, some, sem.at[turn])

    lane = iota((8, LANES), 1)
    lane_f = lane.astype(F32)
    lane16 = iota((16, LANES), 1).astype(jnp.int16)
    last_lane = lane == LANES - 1
    own_row = ((core * XS * ZS + chip) * ROWS_DEV).astype(F32) - (TROWS - 1) / 2.0
    partner_row = (((1 - core) * XS * ZS + chip) * ROWS_DEV).astype(F32) - (TROWS - 1) / 2.0

    def compute(source, part):
        angle = (core * XS * ZS + part * ZS + source) * 2
        spots = part * TILES
        cosine = jnp.where(lower, cos_ref[angle], cos_ref[angle + 1])
        sine = jnp.where(lower, sin_ref[angle], sin_ref[angle + 1])
        values, slopes = [], []
        for pair in range(TILES // 2):
            value_row, slope_row = [], []
            here = [
                [held[source, spots + 2 * pair + half, block].astype(F32) for block in range(KEEP)]
                for half in (0, 1)
            ]
            moved = [[pltpu.roll(v, LANES - 1, 1) for v in row] for row in here]
            for block in range(KEEP):
                diffs = []
                for half in (0, 1):
                    after = moved[half][min(block + 1, KEEP - 1)]
                    diffs.append(
                        jnp.where(last_lane, after, moved[half][block]) - here[half][block]
                    )
                value_row.append(
                    jnp.concatenate([here[0][block], here[1][block]], axis=0).astype(BF16)
                )
                slope_row.append(jnp.concatenate(diffs, axis=0).astype(BF16))
            values.append(value_row)
            slopes.append(slope_row)
        spans, starts = [], []
        for half in (0, 1):
            left_end = half * LANES - (TCOLS - 1) / 2.0
            spans.append((lane_f + left_end) * cosine + float(CENTRE))
            end = jnp.where(cosine >= 0.0, left_end, left_end + LANES - 1.0)
            starts.append(end * cosine + float(CENTRE))
        for row in range(2 * ROWS_DEV):
            y = (partner_row if row < ROWS_DEV else own_row) + float(row % ROWS_DEV)
            lift = sine * y
            for half in (0, 1):
                unit = row * 2 + half
                u = spans[half] + lift
                k = u.astype(jnp.int32)
                part_way = u - k.astype(F32)
                k = k & (LANES - 1)
                index = jnp.concatenate([k, k], axis=0).astype(jnp.int16)
                begin = (starts[half] + lift).astype(jnp.int32)
                begin = jnp.concatenate([begin, begin], axis=0).astype(jnp.int16)
                past0 = begin > lane16
                past1 = begin > lane16 + jnp.int16(LANES)
                for pair in range(TILES // 2):
                    v = values[pair]
                    d = slopes[pair]
                    v = jnp.where(past1, v[2], jnp.where(past0, v[1], v[0]))
                    d = jnp.where(past1, d[2], jnp.where(past0, d[1], d[0]))
                    v = lane_gather(v, index).astype(F32)
                    d = lane_gather(d, index).astype(F32)
                    for half_row in (0, 1):
                        rows = slice(half_row * 8, half_row * 8 + 8)
                        at = slice(pair * 16 + half_row * 8, pair * 16 + half_row * 8 + 8)
                        total[unit, at] += v[rows] + part_way * d[rows]

    @pl.loop(0, ZS + LAG)
    def _(turn):
        @pl.when(turn < ZS)
        def _():
            @pl.when(turn > 0)
            def _():
                column_copy(turn).wait_recv()

            spread(turn)

        @pl.when(turn >= LAG)
        def _():
            ready = turn - LAG
            own_copy(ready).wait()
            all_of_plane(ready, plane_recv).wait()

            @pl.loop(0, XS)
            def _(part):
                compute(slot(ready), part)

    def fold(unit):
        result = []
        for group in range(4):
            pieces = []
            for half in (0, 1):
                v = total[unit, group * 16 + half * 8 : group * 16 + half * 8 + 8]
                pieces.append(v + pltpu.roll(v, 4, 0))
            result.append(jnp.where(lower, pieces[0], pieces[1]))
        return jnp.concatenate(result, axis=0)

    for unit in range(16):
        partner_part[unit] = fold(unit)
    swap = pltpu.make_async_remote_copy(
        src_ref=partner_part,
        dst_ref=arrived_part,
        send_sem=part_send,
        recv_sem=part_recv,
        device_id=partner,
        device_id_type=MESH,
    )
    swap.start()
    for unit in range(16):
        out_ref[0, :, unit * LANES : (unit + 1) * LANES] = fold(unit + 16)
    swap.wait_recv()
    for unit in range(16):
        out_ref[0, :, unit * LANES : (unit + 1) * LANES] += arrived_part[unit]

    swap.wait_send()
    for turn in range(ZS):
        if turn > 0:
            column_copy(turn).wait_send()
        all_of_plane(turn, plane_send).wait()


def body(sinogram, paganin_width, window_block):
    angles = np.pi * np.arange(ANGLES) / ANGLES
    cosines = jnp.asarray(np.cos(angles).astype(np.float32))
    sines = jnp.asarray(np.sin(angles).astype(np.float32))
    smem = pl.BlockSpec(memory_space=pltpu.SMEM)
    vmem = pl.BlockSpec(memory_space=pltpu.VMEM)
    return pl.pallas_call(
        kernel,
        out_shape=jax.ShapeDtypeStruct((1, 32, ROWS_DEV * TCOLS), F32),
        in_specs=[vmem, smem, smem, smem, smem],
        out_specs=vmem,
        scratch_shapes=[
            pltpu.VMEM((272, LANES), F32),
            pltpu.VMEM((272, LANES), F32),
            pltpu.VMEM((BLOCKS - 1, 8, LANES), F32),
            pltpu.VMEM((ZS, TILES, KEEP, 8, LANES), BF16),
            pltpu.VMEM((ZS, XS * TILES, KEEP, 8, LANES), BF16),
            pltpu.VMEM((32, 64, LANES), F32),
            pltpu.VMEM((16, 32, LANES), F32),
            pltpu.VMEM((16, 32, LANES), F32),
            pltpu.SemaphoreType.DMA((ZS,)),
            pltpu.SemaphoreType.DMA((ZS,)),
            pltpu.SemaphoreType.DMA((ZS,)),
            pltpu.SemaphoreType.DMA((ZS,)),
            pltpu.SemaphoreType.DMA((ZS,)),
            pltpu.SemaphoreType.DMA,
            pltpu.SemaphoreType.DMA,
        ],
        compiler_params=pltpu.CompilerParams(collective_id=0, has_side_effects=True),
    )(sinogram, paganin_width, window_block.T, cosines, sines)


def solution(mesh):
    in_specs = (P(("segment", "angle"), "tile", None), P(), P())
    out_specs = P("tile", None, ("segment", "angle"))
    return jax.shard_map(body, mesh=mesh, in_specs=in_specs, out_specs=out_specs, check_vma=False)
```

```python
import functools
import math

import jax
import jax.numpy as jnp
import numpy as np
from jax import lax
from jax.experimental import pallas as pl
from jax.experimental.pallas import tpu as pltpu
from jax.sharding import PartitionSpec as P

MESH = pl.DeviceIdType.MESH
LANES = 128
BAND = 128
ROWS_DEV = 8
TCOLS = 256
ANGLES = 64
TROWS = 256
TILES = 8
ZS = 8
XS = 2
BLOCKS = 32
KEEP = 3
BINS_SHIFT = 64
CENTRE = 256 - BINS_SHIFT
COLUMN = (1, -1, 2, -2)


def ring_distance(step):
    return sum(min(part, 4 - part) for part in step)


PLANE_STEPS = sorted(
    ((a, b) for a in range(4) for b in range(4) if a or b), key=ring_distance, reverse=True
)

F32 = jnp.float32
BF16 = jnp.bfloat16

GATHER = lax.GatherDimensionNumbers(
    offset_dims=(),
    collapsed_slice_dims=(1,),
    start_index_map=(1,),
    operand_batching_dims=(0,),
    start_indices_batching_dims=(0,),
)


def lane_gather(values, index):
    return lax.gather(
        values, index[:, :, None], GATHER, (1, 1), mode=lax.GatherScatterMode.PROMISE_IN_BOUNDS
    )


def iota(shape, axis):
    return lax.broadcasted_iota(jnp.int32, shape, axis)


def split(value):
    high = value.astype(BF16)
    return high, (value - high.astype(F32)).astype(BF16)


def dot3(left, right):
    left_high, left_low = split(left)
    right_high, right_low = split(right)
    return (
        jnp.dot(left_high, right_high, preferred_element_type=F32)
        + jnp.dot(left_low, right_high, preferred_element_type=F32)
        + jnp.dot(left_high, right_low, preferred_element_type=F32)
    )


def smoothing_band(width):
    shape = (3 * LANES, LANES)
    offset = iota(shape, 0) - LANES - iota(shape, 1)
    spread = jnp.abs(offset).astype(F32)
    taps = jnp.exp(-(iota((1, LANES), 1) + 1).astype(F32) / width)
    total = 1.0 + 2.0 * jnp.sum(taps)
    return jnp.where(jnp.abs(offset) <= BAND, jnp.exp(-spread / width) / total, 0.0)


def ramp_band():
    shape = (4 * LANES, LANES)
    offset = iota(shape, 0) - LANES - BINS_SHIFT - iota(shape, 1)
    size = jnp.abs(offset)
    spread = size.astype(F32)
    odd = jnp.where(
        (size <= BAND) & (size % 2 == 1),
        -1.0 / (math.pi * math.pi * jnp.maximum(spread * spread, 1.0)),
        0.0,
    )
    return jnp.where(offset == 0, 0.25, odd)


def filter_rows(sino_ref, width_ref, padded, smooth, filtered):
    zero = jnp.zeros((8, LANES), F32)
    padded[0:8] = zero
    padded[264:272] = zero
    smooth[0:8] = zero
    smooth[264:272] = zero
    for block in range(BLOCKS):
        columns = slice(block * LANES, (block + 1) * LANES)
        padded[(block + 1) * 8 : (block + 2) * 8] = jnp.concatenate(
            [sino_ref[0, :, columns], sino_ref[1, :, columns]], axis=0
        )
    left = jnp.concatenate([padded[8 * k : 8 * k + 256] for k in range(3)], axis=1)
    width = jnp.full((1, 1), width_ref[0], F32)
    smooth[8:264] = dot3(left, smoothing_band(width))
    left = jnp.concatenate([smooth[8 * k : 8 * k + 248] for k in range(4)], axis=1)
    filtered[...] = dot3(left, ramp_band()).reshape(BLOCKS - 1, 8, LANES)


def kernel(
    sino_ref,
    width_ref,
    window_ref,
    cos_ref,
    sin_ref,
    out_ref,
    padded,
    smooth,
    filtered,
    column,
    held,
    total,
    partner_part,
    arrived_part,
    column_send,
    column_recv,
    plane_send,
    plane_recv,
    local_sem,
    part_send,
    part_recv,
):
    core = lax.axis_index("segment")
    chip = lax.axis_index("angle")
    tile = lax.axis_index("tile")
    z = chip % ZS
    spot = (chip // ZS) * TILES + tile
    x = (tile % 2) * 2 + chip // ZS
    y = tile // 2

    def plane_peer(step, rise=0):
        other_x = (x + step[0]) % 4
        other_y = (y + step[1]) % 4
        other_tile = other_y * 2 + other_x // 2
        return other_tile, (core, (other_x % 2) * ZS + (z + rise) % ZS, other_tile)

    def column_peer(rise):
        return (core, chip - z + (z + rise) % ZS, tile)

    partner = (1 - core, chip, tile)

    barrier = pltpu.get_barrier_semaphore()
    for step in PLANE_STEPS:
        pl.semaphore_signal(barrier, inc=1, device_id=plane_peer(step)[1], device_id_type=MESH)
    for rise in COLUMN:
        pl.semaphore_signal(barrier, inc=1, device_id=column_peer(rise), device_id_type=MESH)
    pl.semaphore_signal(barrier, inc=1, device_id=partner, device_id_type=MESH)

    filter_rows(sino_ref, width_ref, padded, smooth, filtered)

    lower = iota((8, LANES), 0) < 4
    first_angle = (core * XS * ZS + chip) * 2
    for other in range(TILES):
        first = window_ref[other, first_angle]
        second = window_ref[other, first_angle + 1]
        for block in range(KEEP):
            column[z, other, block] = jnp.where(
                lower, filtered[first + block], filtered[second + block]
            ).astype(BF16)

    pl.semaphore_wait(barrier, len(PLANE_STEPS) + len(COLUMN) + 1)

    def column_copy(rise):
        return pltpu.make_async_remote_copy(
            src_ref=column.at[z],
            dst_ref=column.at[z],
            send_sem=column_send.at[rise % ZS],
            recv_sem=column_recv.at[rise % ZS],
            device_id=column_peer(rise),
            device_id_type=MESH,
        )

    def slot(shift):
        return (z + ZS - shift) % ZS

    def own_copy(shift):
        return pltpu.make_async_copy(
            column.at[slot(shift), tile], held.at[slot(shift), spot], local_sem.at[shift]
        )

    def spread(shift, rise):
        source = slot(shift)
        arrival = (shift + rise) % ZS
        steps = PLANE_STEPS
        if rise:
            steps = steps + [(0, 0)]
        else:
            own_copy(shift).start()
        for step in steps:
            other_tile, device = plane_peer(step, rise)
            pltpu.make_async_remote_copy(
                src_ref=column.at[source, other_tile],
                dst_ref=held.at[source, spot],
                send_sem=plane_send.at[arrival],
                recv_sem=plane_recv.at[arrival],
                device_id=device,
                device_id_type=MESH,
            ).start()

    def all_of_plane(shift, sem, count):
        some = held.at[slot(shift), pl.ds(0, count)]
        return pltpu.make_async_copy(some, some, sem.at[shift])

    def arrive(shift):
        if shift in (3, 4, 5):
            all_of_plane(shift, plane_recv, XS * TILES).wait()
        else:
            own_copy(shift).wait()
            all_of_plane(shift, plane_recv, XS * TILES - 1).wait()

    for rise in COLUMN:
        column_copy(rise).start()
    spread(0, 0)

    @pl.loop(0, 32)
    def _(unit):
        total[unit] = jnp.zeros((64, LANES), F32)

    for rise in COLUMN[:2]:
        column_copy(rise).wait_recv()
        spread(rise % ZS, 0)
    arrive(0)
    column_copy(2).wait_recv()

    @pl.when(core == 0)
    def _():
        spread(2, 2)

    spread(2, 1)
    column_copy(-2).wait_recv()

    @pl.when(core == 1)
    def _():
        spread(ZS - 2, -2)

    spread(ZS - 2, -1)
    spread(2, 0)
    spread(ZS - 2, 0)

    lane = iota((8, LANES), 1)
    lane_f = lane.astype(F32)
    lane16 = iota((16, LANES), 1).astype(jnp.int16)
    last_lane = lane == LANES - 1
    own_row = ((core * XS * ZS + chip) * ROWS_DEV).astype(F32) - (TROWS - 1) / 2.0
    partner_row = (((1 - core) * XS * ZS + chip) * ROWS_DEV).astype(F32) - (TROWS - 1) / 2.0

    def compute(source, part):
        angle = (core * XS * ZS + part * ZS + source) * 2
        spots = part * TILES
        cosine = jnp.where(lower, cos_ref[angle], cos_ref[angle + 1])
        sine = jnp.where(lower, sin_ref[angle], sin_ref[angle + 1])
        values, slopes = [], []
        for pair in range(TILES // 2):
            value_row, slope_row = [], []
            here = [
                [held[source, spots + 2 * pair + half, block].astype(F32) for block in range(KEEP)]
                for half in (0, 1)
            ]
            moved = [[pltpu.roll(v, LANES - 1, 1) for v in row] for row in here]
            for block in range(KEEP):
                diffs = []
                for half in (0, 1):
                    after = moved[half][min(block + 1, KEEP - 1)]
                    diffs.append(
                        jnp.where(last_lane, after, moved[half][block]) - here[half][block]
                    )
                value_row.append(
                    jnp.concatenate([here[0][block], here[1][block]], axis=0).astype(BF16)
                )
                slope_row.append(jnp.concatenate(diffs, axis=0).astype(BF16))
            values.append(value_row)
            slopes.append(slope_row)
        spans, starts = [], []
        for half in (0, 1):
            left_end = half * LANES - (TCOLS - 1) / 2.0
            spans.append((lane_f + left_end) * cosine + float(CENTRE))
            end = jnp.where(cosine >= 0.0, left_end, left_end + LANES - 1.0)
            starts.append(end * cosine + float(CENTRE))
        for row in range(2 * ROWS_DEV):
            y = (partner_row if row < ROWS_DEV else own_row) + float(row % ROWS_DEV)
            lift = sine * y
            for half in (0, 1):
                unit = row * 2 + half
                u = spans[half] + lift
                k = u.astype(jnp.int32)
                part_way = u - k.astype(F32)
                k = k & (LANES - 1)
                index = jnp.concatenate([k, k], axis=0).astype(jnp.int16)
                begin = (starts[half] + lift).astype(jnp.int32)
                begin = jnp.concatenate([begin, begin], axis=0).astype(jnp.int16)
                past0 = begin > lane16
                past1 = begin > lane16 + jnp.int16(LANES)
                for pair in range(TILES // 2):
                    v = values[pair]
                    d = slopes[pair]
                    v = jnp.where(past1, v[2], jnp.where(past0, v[1], v[0]))
                    d = jnp.where(past1, d[2], jnp.where(past0, d[1], d[0]))
                    v = lane_gather(v, index).astype(F32)
                    d = lane_gather(d, index).astype(F32)
                    for half_row in (0, 1):
                        rows = slice(half_row * 8, half_row * 8 + 8)
                        at = slice(pair * 16 + half_row * 8, pair * 16 + half_row * 8 + 8)
                        total[unit, at] += v[rows] + part_way * d[rows]

    for shift in (0, 1, 7, 2, 6, 3, 5, 4):
        if shift:
            arrive(shift)

        @pl.loop(0, XS)
        def _(part):
            compute(slot(shift), part)

    def fold(unit):
        result = []
        for group in range(4):
            pieces = []
            for half in (0, 1):
                v = total[unit, group * 16 + half * 8 : group * 16 + half * 8 + 8]
                pieces.append(v + pltpu.roll(v, 4, 0))
            result.append(jnp.where(lower, pieces[0], pieces[1]))
        return jnp.concatenate(result, axis=0)

    for unit in range(16):
        partner_part[unit] = fold(unit)
    swap = pltpu.make_async_remote_copy(
        src_ref=partner_part,
        dst_ref=arrived_part,
        send_sem=part_send,
        recv_sem=part_recv,
        device_id=partner,
        device_id_type=MESH,
    )
    swap.start()
    for unit in range(16):
        out_ref[0, :, unit * LANES : (unit + 1) * LANES] = fold(unit + 16)
    swap.wait_recv()
    for unit in range(16):
        out_ref[0, :, unit * LANES : (unit + 1) * LANES] += arrived_part[unit]

    swap.wait_send()
    for rise in COLUMN:
        column_copy(rise).wait_send()
    for shift in range(ZS):
        all_of_plane(shift, plane_send, XS * TILES - (shift not in (3, 4, 5))).wait()


def body(sinogram, paganin_width, window_block):
    angles = np.pi * np.arange(ANGLES) / ANGLES
    cosines = jnp.asarray(np.cos(angles).astype(np.float32))
    sines = jnp.asarray(np.sin(angles).astype(np.float32))
    smem = pl.BlockSpec(memory_space=pltpu.SMEM)
    vmem = pl.BlockSpec(memory_space=pltpu.VMEM)
    return pl.pallas_call(
        kernel,
        out_shape=jax.ShapeDtypeStruct((1, 32, ROWS_DEV * TCOLS), F32),
        in_specs=[vmem, smem, smem, smem, smem],
        out_specs=vmem,
        scratch_shapes=[
            pltpu.VMEM((272, LANES), F32),
            pltpu.VMEM((272, LANES), F32),
            pltpu.VMEM((BLOCKS - 1, 8, LANES), F32),
            pltpu.VMEM((ZS, TILES, KEEP, 8, LANES), BF16),
            pltpu.VMEM((ZS, XS * TILES, KEEP, 8, LANES), BF16),
            pltpu.VMEM((32, 64, LANES), F32),
            pltpu.VMEM((16, 32, LANES), F32),
            pltpu.VMEM((16, 32, LANES), F32),
            pltpu.SemaphoreType.DMA((ZS,)),
            pltpu.SemaphoreType.DMA((ZS,)),
            pltpu.SemaphoreType.DMA((ZS,)),
            pltpu.SemaphoreType.DMA((ZS,)),
            pltpu.SemaphoreType.DMA((ZS,)),
            pltpu.SemaphoreType.DMA,
            pltpu.SemaphoreType.DMA,
        ],
        compiler_params=pltpu.CompilerParams(collective_id=0, has_side_effects=True),
    )(sinogram, paganin_width, window_block.T, cosines, sines)


def solution(mesh):
    in_specs = (P(("segment", "angle"), "tile", None), P(), P())
    out_specs = P("tile", None, ("segment", "angle"))
    return jax.shard_map(body, mesh=mesh, in_specs=in_specs, out_specs=out_specs, check_vma=False)
```

```python
import functools
import math

import jax
import jax.numpy as jnp
import numpy as np
from jax import lax
from jax.experimental import pallas as pl
from jax.experimental.pallas import tpu as pltpu
from jax.sharding import PartitionSpec as P

MESH = pl.DeviceIdType.MESH
LANES = 128
BAND = 128
ROWS_DEV = 8
TCOLS = 256
ANGLES = 64
TROWS = 256
TILES = 8
ZS = 8
XS = 2
BLOCKS = 32
KEEP = 3
BINS_SHIFT = 64
CENTRE = 256 - BINS_SHIFT
COLUMN = (1, -1, 2, -2)
ORDER = (0, 1, 7, 4, 3, 5, 2, 6)


def ring_distance(step):
    return sum(min(part, 4 - part) for part in step)


PLANE_STEPS = sorted(
    ((a, b) for a in range(4) for b in range(4) if a or b), key=ring_distance, reverse=True
)

F32 = jnp.float32
BF16 = jnp.bfloat16

GATHER = lax.GatherDimensionNumbers(
    offset_dims=(),
    collapsed_slice_dims=(1,),
    start_index_map=(1,),
    operand_batching_dims=(0,),
    start_indices_batching_dims=(0,),
)


def lane_gather(values, index):
    return lax.gather(
        values, index[:, :, None], GATHER, (1, 1), mode=lax.GatherScatterMode.PROMISE_IN_BOUNDS
    )


def iota(shape, axis):
    return lax.broadcasted_iota(jnp.int32, shape, axis)


def split(value):
    high = value.astype(BF16)
    return high, (value - high.astype(F32)).astype(BF16)


def dot3(left, right):
    left_high, left_low = split(left)
    right_high, right_low = split(right)
    return (
        jnp.dot(left_high, right_high, preferred_element_type=F32)
        + jnp.dot(left_low, right_high, preferred_element_type=F32)
        + jnp.dot(left_high, right_low, preferred_element_type=F32)
    )


def smoothing_band(width):
    shape = (3 * LANES, LANES)
    offset = iota(shape, 0) - LANES - iota(shape, 1)
    spread = jnp.abs(offset).astype(F32)
    taps = jnp.exp(-(iota((1, LANES), 1) + 1).astype(F32) / width)
    total = 1.0 + 2.0 * jnp.sum(taps)
    return jnp.where(jnp.abs(offset) <= BAND, jnp.exp(-spread / width) / total, 0.0)


def ramp_band():
    shape = (4 * LANES, LANES)
    offset = iota(shape, 0) - LANES - BINS_SHIFT - iota(shape, 1)
    size = jnp.abs(offset)
    spread = size.astype(F32)
    odd = jnp.where(
        (size <= BAND) & (size % 2 == 1),
        -1.0 / (math.pi * math.pi * jnp.maximum(spread * spread, 1.0)),
        0.0,
    )
    return jnp.where(offset == 0, 0.25, odd)


def filter_rows(sino_ref, width_ref, padded, smooth, filtered):
    zero = jnp.zeros((8, LANES), F32)
    padded[0:8] = zero
    padded[264:272] = zero
    smooth[0:8] = zero
    smooth[264:272] = zero
    for block in range(BLOCKS):
        columns = slice(block * LANES, (block + 1) * LANES)
        padded[(block + 1) * 8 : (block + 2) * 8] = jnp.concatenate(
            [sino_ref[0, :, columns], sino_ref[1, :, columns]], axis=0
        )
    left = jnp.concatenate([padded[8 * k : 8 * k + 256] for k in range(3)], axis=1)
    width = jnp.full((1, 1), width_ref[0], F32)
    smooth[8:264] = dot3(left, smoothing_band(width))
    left = jnp.concatenate([smooth[8 * k : 8 * k + 248] for k in range(4)], axis=1)
    filtered[...] = dot3(left, ramp_band()).reshape(BLOCKS - 1, 8, LANES)


def kernel(
    sino_ref,
    width_ref,
    window_ref,
    cos_ref,
    sin_ref,
    out_ref,
    arrived_part,
    padded,
    smooth,
    filtered,
    column,
    held,
    total,
    partner_part,
    index_table,
    start_table,
    fraction_table,
    column_send,
    column_recv,
    plane_send,
    plane_recv,
    local_sem,
    part_send,
    part_recv,
):
    core = lax.axis_index("segment")
    chip = lax.axis_index("angle")
    tile = lax.axis_index("tile")
    z = chip % ZS
    spot = (chip // ZS) * TILES + tile
    x = (tile % 2) * 2 + chip // ZS
    y = tile // 2

    def plane_peer(step, rise=0):
        other_x = (x + step[0]) % 4
        other_y = (y + step[1]) % 4
        other_tile = other_y * 2 + other_x // 2
        return other_tile, (core, (other_x % 2) * ZS + (z + rise) % ZS, other_tile)

    def column_peer(rise):
        return (core, chip - z + (z + rise) % ZS, tile)

    partner = (1 - core, chip, tile)

    barrier = pltpu.get_barrier_semaphore()
    for step in PLANE_STEPS:
        pl.semaphore_signal(barrier, inc=1, device_id=plane_peer(step)[1], device_id_type=MESH)
    for rise in COLUMN:
        pl.semaphore_signal(barrier, inc=1, device_id=column_peer(rise), device_id_type=MESH)
    pl.semaphore_signal(barrier, inc=1, device_id=partner, device_id_type=MESH)

    filter_rows(sino_ref, width_ref, padded, smooth, filtered)

    lower = iota((8, LANES), 0) < 4
    first_angle = (core * XS * ZS + chip) * 2
    for other in range(TILES):
        first = window_ref[other, first_angle]
        second = window_ref[other, first_angle + 1]
        for block in range(KEEP):
            column[z, other, block] = jnp.where(
                lower, filtered[first + block], filtered[second + block]
            ).astype(BF16)

    pl.semaphore_wait(barrier, len(PLANE_STEPS) + len(COLUMN) + 1)

    def column_copy(rise):
        return pltpu.make_async_remote_copy(
            src_ref=column.at[z],
            dst_ref=column.at[z],
            send_sem=column_send.at[rise % ZS],
            recv_sem=column_recv.at[rise % ZS],
            device_id=column_peer(rise),
            device_id_type=MESH,
        )

    def slot(shift):
        return (z + ZS - shift) % ZS

    def own_copy(shift):
        return pltpu.make_async_copy(
            column.at[slot(shift), tile], held.at[slot(shift), spot], local_sem.at[shift]
        )

    def spread(shift, rise):
        source = slot(shift)
        arrival = (shift + rise) % ZS
        steps = PLANE_STEPS
        if rise:
            steps = steps + [(0, 0)]
        else:
            own_copy(shift).start()
        for step in steps:
            other_tile, device = plane_peer(step, rise)
            pltpu.make_async_remote_copy(
                src_ref=column.at[source, other_tile],
                dst_ref=held.at[source, spot],
                send_sem=plane_send.at[arrival],
                recv_sem=plane_recv.at[arrival],
                device_id=device,
                device_id_type=MESH,
            ).start()

    def all_of_plane(shift, sem, count):
        some = held.at[slot(shift), pl.ds(0, count)]
        return pltpu.make_async_copy(some, some, sem.at[shift])

    def arrive(shift):
        if shift in (3, 4, 5):
            all_of_plane(shift, plane_recv, XS * TILES).wait()
        else:
            own_copy(shift).wait()
            all_of_plane(shift, plane_recv, XS * TILES - 1).wait()

    for rise in COLUMN:
        column_copy(rise).start()
    spread(0, 0)

    lane_f = iota((8, LANES), 1).astype(F32)
    lane16 = iota((16, LANES), 1).astype(jnp.int16)
    last_lane = lane16 == jnp.int16(LANES - 1)
    own_row = ((core * XS * ZS + chip) * ROWS_DEV).astype(F32) - (TROWS - 1) / 2.0
    partner_row = (((1 - core) * XS * ZS + chip) * ROWS_DEV).astype(F32) - (TROWS - 1) / 2.0

    @pl.loop(0, XS * ZS)
    def _(which):
        angle = (core * XS * ZS + which) * 2
        cosine = jnp.where(lower, cos_ref[angle], cos_ref[angle + 1])
        sine = jnp.where(lower, sin_ref[angle], sin_ref[angle + 1])
        spans, starts = [], []
        for half in (0, 1):
            left_end = half * LANES - (TCOLS - 1) / 2.0
            spans.append((lane_f + left_end) * cosine + float(CENTRE))
            end = jnp.where(cosine >= 0.0, left_end, left_end + LANES - 1.0)
            starts.append(end * cosine + float(CENTRE))
        for row in range(2 * ROWS_DEV):
            y = (partner_row if row < ROWS_DEV else own_row) + float(row % ROWS_DEV)
            lift = sine * y
            for half in (0, 1):
                unit = row * 2 + half
                u = spans[half] + lift
                k = u.astype(jnp.int32)
                fraction_table[which, unit] = u - k.astype(F32)
                k = k & (LANES - 1)
                index_table[which, unit] = jnp.concatenate([k, k], axis=0).astype(jnp.int16)
                begin = (starts[half] + lift).astype(jnp.int32)
                start_table[which, unit] = jnp.concatenate([begin, begin], axis=0).astype(
                    jnp.int16
                )

    def sources(source, part):
        values, slopes = [], []
        for pair in range(TILES // 2):
            first = part * TILES + 2 * pair
            here = [
                jnp.concatenate(
                    [held[source, first, block], held[source, first + 1, block]], axis=0
                )
                for block in range(KEEP)
            ]
            moved = [pltpu.roll(v, LANES - 1, 1) for v in here]
            values.append(here)
            slopes.append(
                [
                    jnp.where(last_lane, moved[min(block + 1, KEEP - 1)], moved[block])
                    - here[block]
                    for block in range(KEEP)
                ]
            )
        return values, slopes

    def compute(source, part, units, fresh=False):
        which = part * ZS + source
        values, slopes = sources(source, part)
        for unit in units:
            index = index_table[which, unit]
            begin = start_table[which, unit]
            part_way = fraction_table[which, unit]
            past0 = begin > lane16
            past1 = begin > lane16 + jnp.int16(LANES)
            for pair in range(TILES // 2):
                v = values[pair]
                d = slopes[pair]
                v = jnp.where(past1, v[2], jnp.where(past0, v[1], v[0]))
                d = jnp.where(past1, d[2], jnp.where(past0, d[1], d[0]))
                v = lane_gather(v, index).astype(F32)
                d = lane_gather(d, index).astype(F32)
                for half_row in (0, 1):
                    rows = slice(half_row * 8, half_row * 8 + 8)
                    at = slice(pair * 16 + half_row * 8, pair * 16 + half_row * 8 + 8)
                    term = v[rows] + part_way * d[rows]
                    if fresh:
                        total[unit, at] = term
                    else:
                        total[unit, at] += term

    for rise in COLUMN[:2]:
        column_copy(rise).wait_recv()
        spread(rise % ZS, 0)
    arrive(0)
    column_copy(2).wait_recv()

    @pl.when(core == 0)
    def _():
        spread(2, 2)

    spread(2, 1)
    column_copy(-2).wait_recv()

    @pl.when(core == 1)
    def _():
        spread(ZS - 2, -2)

    spread(ZS - 2, -1)
    spread(2, 0)
    spread(ZS - 2, 0)

    def fold(unit):
        result = []
        for group in range(4):
            pieces = []
            for half in (0, 1):
                v = total[unit, group * 16 + half * 8 : group * 16 + half * 8 + 8]
                pieces.append(v + pltpu.roll(v, 4, 0))
            result.append(jnp.where(lower, pieces[0], pieces[1]))
        return jnp.concatenate(result, axis=0)

    theirs, ours = range(16), range(16, 32)
    for shift in ORDER[:-1]:
        if shift:
            arrive(shift)
        for part in range(XS):
            compute(slot(shift), part, range(32), fresh=shift == 0 and part == 0)

    arrive(ORDER[-1])
    for part in range(XS):
        compute(slot(ORDER[-1]), part, theirs)
    for unit in theirs:
        partner_part[0, :, unit * LANES : (unit + 1) * LANES] = fold(unit)
    swap = pltpu.make_async_remote_copy(
        src_ref=partner_part,
        dst_ref=arrived_part,
        send_sem=part_send,
        recv_sem=part_recv,
        device_id=partner,
        device_id_type=MESH,
    )
    swap.start()
    for part in range(XS):
        compute(slot(ORDER[-1]), part, ours)
    for unit in ours:
        out_ref[0, :, (unit - 16) * LANES : (unit - 15) * LANES] = fold(unit)
    swap.wait()
    for rise in COLUMN:
        column_copy(rise).wait_send()
    for shift in range(ZS):
        all_of_plane(shift, plane_send, XS * TILES - (shift not in (3, 4, 5))).wait()


def body(sinogram, paganin_width, window_block):
    angles = np.pi * np.arange(ANGLES) / ANGLES
    cosines = jnp.asarray(np.cos(angles).astype(np.float32))
    sines = jnp.asarray(np.sin(angles).astype(np.float32))
    smem = pl.BlockSpec(memory_space=pltpu.SMEM)
    vmem = pl.BlockSpec(memory_space=pltpu.VMEM)
    part = jax.ShapeDtypeStruct((1, 32, ROWS_DEV * TCOLS), F32)
    own, arrived = pl.pallas_call(
        kernel,
        out_shape=(part, part),
        in_specs=[vmem, smem, smem, smem, smem],
        out_specs=(vmem, vmem),
        scratch_shapes=[
            pltpu.VMEM((272, LANES), F32),
            pltpu.VMEM((272, LANES), F32),
            pltpu.VMEM((BLOCKS - 1, 8, LANES), F32),
            pltpu.VMEM((ZS, TILES, KEEP, 8, LANES), BF16),
            pltpu.VMEM((ZS, XS * TILES, KEEP, 8, LANES), BF16),
            pltpu.VMEM((32, 64, LANES), F32),
            pltpu.VMEM((1, 32, ROWS_DEV * TCOLS), F32),
            pltpu.VMEM((XS * ZS, 32, 16, LANES), jnp.int16),
            pltpu.VMEM((XS * ZS, 32, 16, LANES), jnp.int16),
            pltpu.VMEM((XS * ZS, 32, 8, LANES), F32),
            pltpu.SemaphoreType.DMA((ZS,)),
            pltpu.SemaphoreType.DMA((ZS,)),
            pltpu.SemaphoreType.DMA((ZS,)),
            pltpu.SemaphoreType.DMA((ZS,)),
            pltpu.SemaphoreType.DMA((ZS,)),
            pltpu.SemaphoreType.DMA,
            pltpu.SemaphoreType.DMA,
        ],
        compiler_params=pltpu.CompilerParams(
            collective_id=0, has_side_effects=True, vmem_limit_bytes=32 << 20
        ),
    )(sinogram, paganin_width, window_block.T, cosines, sines)
    return own + arrived


def solution(mesh):
    in_specs = (P(("segment", "angle"), "tile", None), P(), P())
    out_specs = P("tile", None, ("segment", "angle"))
    return jax.shard_map(body, mesh=mesh, in_specs=in_specs, out_specs=out_specs, check_vma=False)
```

```python
import functools
import math

import jax
import jax.numpy as jnp
from jax import lax
from jax.experimental import pallas as pl
from jax.experimental.pallas import tpu as pltpu
from jax.sharding import PartitionSpec as P

MESH = pl.DeviceIdType.MESH
LANES = 128
BAND = 128
ROWS_DEV = 8
TCOLS = 256
ANGLES = 64
TROWS = 256
TILES = 8
ZS = 8
XS = 2
BLOCKS = 32
KEEP = 3
BINS_SHIFT = 64
CENTRE = 256 - BINS_SHIFT
COLUMN = (1, -1, 2, -2)
ORDER = (0, 1, 7, 4, 3, 5, 2, 6)


def ring_distance(step):
    return sum(min(part, 4 - part) for part in step)


PLANE_STEPS = sorted(
    ((a, b) for a in range(4) for b in range(4) if a or b), key=ring_distance, reverse=True
)

F32 = jnp.float32
BF16 = jnp.bfloat16

GATHER = lax.GatherDimensionNumbers(
    offset_dims=(),
    collapsed_slice_dims=(1,),
    start_index_map=(1,),
    operand_batching_dims=(0,),
    start_indices_batching_dims=(0,),
)


def lane_gather(values, index):
    return lax.gather(
        values, index[:, :, None], GATHER, (1, 1), mode=lax.GatherScatterMode.PROMISE_IN_BOUNDS
    )


def iota(shape, axis):
    return lax.broadcasted_iota(jnp.int32, shape, axis)


def split(value):
    high = value.astype(BF16)
    return high, (value - high.astype(F32)).astype(BF16)


def dot3(left, right):
    left_high, left_low = split(left)
    right_high, right_low = split(right)
    return (
        jnp.dot(left_high, right_high, preferred_element_type=F32)
        + jnp.dot(left_low, right_high, preferred_element_type=F32)
        + jnp.dot(left_high, right_low, preferred_element_type=F32)
    )


def smoothing_band(width):
    shape = (3 * LANES, LANES)
    offset = iota(shape, 0) - LANES - iota(shape, 1)
    spread = jnp.abs(offset).astype(F32)
    taps = jnp.exp(-(iota((1, LANES), 1) + 1).astype(F32) / width)
    total = 1.0 + 2.0 * jnp.sum(taps)
    return jnp.where(jnp.abs(offset) <= BAND, jnp.exp(-spread / width) / total, 0.0)


def ramp_band():
    shape = (4 * LANES, LANES)
    offset = iota(shape, 0) - LANES - BINS_SHIFT - iota(shape, 1)
    size = jnp.abs(offset)
    spread = size.astype(F32)
    odd = jnp.where(
        (size <= BAND) & (size % 2 == 1),
        -1.0 / (math.pi * math.pi * jnp.maximum(spread * spread, 1.0)),
        0.0,
    )
    return jnp.where(offset == 0, 0.25, odd)


def filter_rows(sino_copy, sino_ref, width_ref, padded, smooth, filtered):
    smoothing = smoothing_band(jnp.full((1, 1), width_ref[0], F32))
    ramp = ramp_band()
    zero = jnp.zeros((8, LANES), F32)
    padded[0:8] = zero
    padded[264:272] = zero
    smooth[0:8] = zero
    smooth[264:272] = zero
    sino_copy.wait()
    for block in range(BLOCKS):
        columns = slice(block * LANES, (block + 1) * LANES)
        padded[(block + 1) * 8 : (block + 2) * 8] = jnp.concatenate(
            [sino_ref[0, :, columns], sino_ref[1, :, columns]], axis=0
        )
    left = jnp.concatenate([padded[8 * k : 8 * k + 256] for k in range(3)], axis=1)
    smooth[8:264] = dot3(left, smoothing)
    left = jnp.concatenate([smooth[8 * k : 8 * k + 248] for k in range(4)], axis=1)
    filtered[...] = dot3(left, ramp).reshape(BLOCKS - 1, 8, LANES)


def kernel(
    sino_hbm,
    width_ref,
    window_hbm,
    out_ref,
    arrived_part,
    sino_ref,
    window_ref,
    padded,
    smooth,
    filtered,
    column,
    held,
    total,
    partner_part,
    index_table,
    start_table,
    fraction_table,
    input_sem,
    column_send,
    column_recv,
    plane_send,
    plane_recv,
    local_sem,
    part_send,
    part_recv,
):
    sino_copy = pltpu.make_async_copy(sino_hbm, sino_ref, input_sem.at[0])
    window_copy = pltpu.make_async_copy(window_hbm, window_ref, input_sem.at[1])
    sino_copy.start()
    window_copy.start()
    core = lax.axis_index("segment")
    chip = lax.axis_index("angle")
    tile = lax.axis_index("tile")
    z = chip % ZS
    spot = (chip // ZS) * TILES + tile
    x = (tile % 2) * 2 + chip // ZS
    y = tile // 2

    def plane_peer(step, rise=0):
        other_x = (x + step[0]) % 4
        other_y = (y + step[1]) % 4
        other_tile = other_y * 2 + other_x // 2
        return other_tile, (core, (other_x % 2) * ZS + (z + rise) % ZS, other_tile)

    def column_peer(rise):
        return (core, chip - z + (z + rise) % ZS, tile)

    partner = (1 - core, chip, tile)

    barrier = pltpu.get_barrier_semaphore()
    for step in PLANE_STEPS:
        pl.semaphore_signal(barrier, inc=1, device_id=plane_peer(step)[1], device_id_type=MESH)
    for rise in COLUMN:
        pl.semaphore_signal(barrier, inc=1, device_id=column_peer(rise), device_id_type=MESH)
    pl.semaphore_signal(barrier, inc=1, device_id=partner, device_id_type=MESH)

    filter_rows(sino_copy, sino_ref, width_ref, padded, smooth, filtered)
    window_copy.wait()

    lower = iota((8, LANES), 0) < 4
    first_angle = (core * XS * ZS + chip) * 2
    for other in range(TILES):
        first = window_ref[other, first_angle]
        second = window_ref[other, first_angle + 1]
        for block in range(KEEP):
            column[z, other, block] = jnp.where(
                lower, filtered[first + block], filtered[second + block]
            ).astype(BF16)

    pl.semaphore_wait(barrier, len(PLANE_STEPS) + len(COLUMN) + 1)

    def column_copy(rise):
        return pltpu.make_async_remote_copy(
            src_ref=column.at[z],
            dst_ref=column.at[z],
            send_sem=column_send.at[rise % ZS],
            recv_sem=column_recv.at[rise % ZS],
            device_id=column_peer(rise),
            device_id_type=MESH,
        )

    def slot(shift):
        return (z + ZS - shift) % ZS

    def own_copy(shift):
        return pltpu.make_async_copy(
            column.at[slot(shift), tile], held.at[slot(shift), spot], local_sem.at[shift]
        )

    def spread(shift, rise):
        source = slot(shift)
        arrival = (shift + rise) % ZS
        steps = PLANE_STEPS
        if rise:
            steps = steps + [(0, 0)]
        else:
            own_copy(shift).start()
        for step in steps:
            other_tile, device = plane_peer(step, rise)
            pltpu.make_async_remote_copy(
                src_ref=column.at[source, other_tile],
                dst_ref=held.at[source, spot],
                send_sem=plane_send.at[arrival],
                recv_sem=plane_recv.at[arrival],
                device_id=device,
                device_id_type=MESH,
            ).start()

    def all_of_plane(shift, sem, count):
        some = held.at[slot(shift), pl.ds(0, count)]
        return pltpu.make_async_copy(some, some, sem.at[shift])

    def arrive(shift):
        if shift in (3, 4, 5):
            all_of_plane(shift, plane_recv, XS * TILES).wait()
        else:
            own_copy(shift).wait()
            all_of_plane(shift, plane_recv, XS * TILES - 1).wait()

    for rise in COLUMN:
        column_copy(rise).start()
    spread(0, 0)

    lane_f = iota((8, LANES), 1).astype(F32)
    lane16 = iota((16, LANES), 1).astype(jnp.int16)
    last_lane = lane16 == jnp.int16(LANES - 1)
    own_row = ((core * XS * ZS + chip) * ROWS_DEV).astype(F32) - (TROWS - 1) / 2.0
    partner_row = (((1 - core) * XS * ZS + chip) * ROWS_DEV).astype(F32) - (TROWS - 1) / 2.0

    @pl.loop(0, XS * ZS)
    def _(which):
        angle = (core * XS * ZS + which) * 2
        theta = jnp.where(lower, angle, angle + 1).astype(F32) * (math.pi / ANGLES)
        cosine, sine = jnp.cos(theta), jnp.sin(theta)
        spans, starts = [], []
        for half in (0, 1):
            left_end = half * LANES - (TCOLS - 1) / 2.0
            spans.append((lane_f + left_end) * cosine + float(CENTRE))
            end = jnp.where(cosine >= 0.0, left_end, left_end + LANES - 1.0)
            starts.append(end * cosine + float(CENTRE))
        for row in range(2 * ROWS_DEV):
            y = (partner_row if row < ROWS_DEV else own_row) + float(row % ROWS_DEV)
            lift = sine * y
            for half in (0, 1):
                unit = row * 2 + half
                u = spans[half] + lift
                k = u.astype(jnp.int32)
                fraction_table[which, unit] = u - k.astype(F32)
                index_table[which, unit] = k & (LANES - 1)
                start_table[which, unit] = (starts[half] + lift).astype(jnp.int32)

    def compute(source, part, units):
        which = part * ZS + source
        values, slopes = [], []
        for pair in range(TILES // 2):
            first = part * TILES + 2 * pair
            here = [
                jnp.concatenate(
                    [
                        held[source, first, block].astype(F32),
                        held[source, first + 1, block].astype(F32),
                    ],
                    axis=0,
                ).astype(BF16)
                for block in range(KEEP)
            ]
            moved = [pltpu.roll(v, LANES - 1, 1) for v in here]
            values.append(here)
            slopes.append(
                [
                    jnp.where(last_lane, moved[min(block + 1, KEEP - 1)], moved[block])
                    - here[block]
                    for block in range(KEEP)
                ]
            )
        for unit in units:
            index = index_table[which, unit]
            index = jnp.concatenate([index, index], axis=0).astype(jnp.int16)
            begin = start_table[which, unit]
            begin = jnp.concatenate([begin, begin], axis=0).astype(jnp.int16)
            part_way = fraction_table[which, unit]
            past0 = begin > lane16
            past1 = begin > lane16 + jnp.int16(LANES)
            for pair in range(TILES // 2):
                v = values[pair]
                d = slopes[pair]
                v = jnp.where(past1, v[2], jnp.where(past0, v[1], v[0]))
                d = jnp.where(past1, d[2], jnp.where(past0, d[1], d[0]))
                v = lane_gather(v, index).astype(F32)
                d = lane_gather(d, index).astype(F32)
                for half_row in (0, 1):
                    rows = slice(half_row * 8, half_row * 8 + 8)
                    at = slice(pair * 16 + half_row * 8, pair * 16 + half_row * 8 + 8)
                    term = v[rows] + part_way * d[rows]
                    total[unit, at] += term

    for rise in COLUMN[:2]:
        column_copy(rise).wait_recv()
        spread(rise % ZS, 0)
    arrive(0)
    column_copy(2).wait_recv()

    @pl.when(core == 0)
    def _():
        spread(2, 2)

    spread(2, 1)
    column_copy(-2).wait_recv()

    @pl.when(core == 1)
    def _():
        spread(ZS - 2, -2)

    spread(ZS - 2, -1)
    spread(2, 0)
    spread(ZS - 2, 0)

    def fold(unit):
        result = []
        for group in range(4):
            pieces = []
            for half in (0, 1):
                v = total[unit, group * 16 + half * 8 : group * 16 + half * 8 + 8]
                pieces.append(v + pltpu.roll(v, 4, 0))
            result.append(jnp.where(lower, pieces[0], pieces[1]))
        return jnp.concatenate(result, axis=0)

    def run(source, units):
        for part in range(XS):
            compute(source, part, units)

    @pl.loop(0, 32)
    def _(unit):
        total[unit] = jnp.zeros((64, LANES), F32)

    theirs, ours = range(16), range(16, 32)
    for shift in ORDER[:-1]:
        if shift:
            arrive(shift)
        run(slot(shift), range(32))

    arrive(ORDER[-1])
    run(slot(ORDER[-1]), theirs)
    for unit in theirs:
        partner_part[0, :, unit * LANES : (unit + 1) * LANES] = fold(unit)
    swap = pltpu.make_async_remote_copy(
        src_ref=partner_part,
        dst_ref=arrived_part,
        send_sem=part_send,
        recv_sem=part_recv,
        device_id=partner,
        device_id_type=MESH,
    )
    swap.start()
    run(slot(ORDER[-1]), ours)
    for unit in ours:
        out_ref[0, :, (unit - 16) * LANES : (unit - 15) * LANES] = fold(unit)
    swap.wait()
    for rise in COLUMN:
        column_copy(rise).wait_send()
    for shift in range(ZS):
        all_of_plane(shift, plane_send, XS * TILES - (shift not in (3, 4, 5))).wait()


def body(sinogram, paganin_width, window_block):
    smem = pl.BlockSpec(memory_space=pltpu.SMEM)
    hbm = pl.BlockSpec(memory_space=pltpu.HBM)
    vmem = pl.BlockSpec(memory_space=pltpu.VMEM)
    part = jax.ShapeDtypeStruct((1, 32, ROWS_DEV * TCOLS), F32)
    own, arrived = pl.pallas_call(
        kernel,
        out_shape=(part, part),
        in_specs=[hbm, smem, hbm],
        out_specs=(vmem, vmem),
        scratch_shapes=[
            pltpu.VMEM((2, 4, BLOCKS * LANES), F32),
            pltpu.SMEM((TILES, ANGLES), jnp.int32),
            pltpu.VMEM((272, LANES), F32),
            pltpu.VMEM((272, LANES), F32),
            pltpu.VMEM((BLOCKS - 1, 8, LANES), F32),
            pltpu.VMEM((ZS, TILES, KEEP, 8, LANES), BF16),
            pltpu.VMEM((ZS, XS * TILES, KEEP, 8, LANES), BF16),
            pltpu.VMEM((32, 64, LANES), F32),
            pltpu.VMEM((1, 32, ROWS_DEV * TCOLS), F32),
            pltpu.VMEM((XS * ZS, 32, 8, LANES), jnp.int32),
            pltpu.VMEM((XS * ZS, 32, 8, LANES), jnp.int32),
            pltpu.VMEM((XS * ZS, 32, 8, LANES), F32),
            pltpu.SemaphoreType.DMA((2,)),
            pltpu.SemaphoreType.DMA((ZS,)),
            pltpu.SemaphoreType.DMA((ZS,)),
            pltpu.SemaphoreType.DMA((ZS,)),
            pltpu.SemaphoreType.DMA((ZS,)),
            pltpu.SemaphoreType.DMA((ZS,)),
            pltpu.SemaphoreType.DMA,
            pltpu.SemaphoreType.DMA,
        ],
        compiler_params=pltpu.CompilerParams(
            collective_id=0, has_side_effects=True, vmem_limit_bytes=32 << 20
        ),
    )(sinogram, paganin_width, window_block.T)
    return own + arrived


def solution(mesh):
    in_specs = (P(("segment", "angle"), "tile", None), P(), P())
    out_specs = P("tile", None, ("segment", "angle"))
    return jax.shard_map(body, mesh=mesh, in_specs=in_specs, out_specs=out_specs, check_vma=False)
```

```python
import functools
import math

import jax
import jax.numpy as jnp
from jax import lax
from jax.experimental import pallas as pl
from jax.experimental.pallas import tpu as pltpu
from jax.sharding import PartitionSpec as P

MESH = pl.DeviceIdType.MESH
LANES = 128
BAND = 128
ROWS_DEV = 8
TCOLS = 256
ANGLES = 64
TROWS = 256
TILES = 8
ZS = 8
XS = 2
BLOCKS = 32
KEEP = 3
BINS_SHIFT = 64
CENTRE = 256 - BINS_SHIFT
COLUMN = (1, -1, 2, -2)
ORDER = (0, 1, 7, 4, 3, 5, 2, 6)


def ring_distance(step):
    return sum(min(part, 4 - part) for part in step)


PLANE_STEPS = sorted(
    ((a, b) for a in range(4) for b in range(4) if a or b), key=ring_distance, reverse=True
)

F32 = jnp.float32
BF16 = jnp.bfloat16

GATHER = lax.GatherDimensionNumbers(
    offset_dims=(),
    collapsed_slice_dims=(1,),
    start_index_map=(1,),
    operand_batching_dims=(0,),
    start_indices_batching_dims=(0,),
)


def lane_gather(values, index):
    return lax.gather(
        values, index[:, :, None], GATHER, (1, 1), mode=lax.GatherScatterMode.PROMISE_IN_BOUNDS
    )


def iota(shape, axis):
    return lax.broadcasted_iota(jnp.int32, shape, axis)


def split(value):
    high = value.astype(BF16)
    return high, (value - high.astype(F32)).astype(BF16)


def dot3(left, right):
    left_high, left_low = split(left)
    right_high, right_low = split(right)
    return (
        jnp.dot(left_high, right_high, preferred_element_type=F32)
        + jnp.dot(left_low, right_high, preferred_element_type=F32)
        + jnp.dot(left_high, right_low, preferred_element_type=F32)
    )


def smoothing_band(width):
    shape = (3 * LANES, LANES)
    offset = iota(shape, 0) - LANES - iota(shape, 1)
    spread = jnp.abs(offset).astype(F32)
    taps = jnp.exp(-(iota((1, LANES), 1) + 1).astype(F32) / width)
    total = 1.0 + 2.0 * jnp.sum(taps)
    return jnp.where(jnp.abs(offset) <= BAND, jnp.exp(-spread / width) / total, 0.0)


def ramp_band():
    shape = (4 * LANES, LANES)
    offset = iota(shape, 0) - LANES - BINS_SHIFT - iota(shape, 1)
    size = jnp.abs(offset)
    spread = size.astype(F32)
    odd = jnp.where(
        (size <= BAND) & (size % 2 == 1),
        -1.0 / (math.pi * math.pi * jnp.maximum(spread * spread, 1.0)),
        0.0,
    )
    return jnp.where(offset == 0, 0.25, odd)


def filter_rows(sino_copy, sino_ref, width_ref, padded, smooth, filtered):
    smoothing = smoothing_band(jnp.full((1, 1), width_ref[0], F32))
    ramp = ramp_band()
    zero = jnp.zeros((8, LANES), F32)
    padded[0:8] = zero
    padded[264:272] = zero
    smooth[0:8] = zero
    smooth[264:272] = zero
    sino_copy.wait()
    for block in range(BLOCKS):
        columns = slice(block * LANES, (block + 1) * LANES)
        padded[(block + 1) * 8 : (block + 2) * 8] = jnp.concatenate(
            [sino_ref[0, :, columns], sino_ref[1, :, columns]], axis=0
        )
    left = jnp.concatenate([padded[8 * k : 8 * k + 256] for k in range(3)], axis=1)
    smooth[8:264] = dot3(left, smoothing)
    left = jnp.concatenate([smooth[8 * k : 8 * k + 248] for k in range(4)], axis=1)
    filtered[...] = dot3(left, ramp).reshape(BLOCKS - 1, 8, LANES)


def kernel(
    sino_hbm,
    width_ref,
    window_hbm,
    out_ref,
    arrived_part,
    sino_ref,
    window_ref,
    padded,
    smooth,
    filtered,
    column,
    held,
    total,
    partner_part,
    index_table,
    start_table,
    fraction_table,
    input_sem,
    column_send,
    column_recv,
    plane_send,
    plane_recv,
    local_sem,
    part_send,
    part_recv,
):
    sino_copy = pltpu.make_async_copy(sino_hbm, sino_ref, input_sem.at[0])
    window_copy = pltpu.make_async_copy(window_hbm, window_ref, input_sem.at[1])
    sino_copy.start()
    window_copy.start()
    core = lax.axis_index("segment")
    chip = lax.axis_index("angle")
    tile = lax.axis_index("tile")
    z = chip % ZS
    spot = (chip // ZS) * TILES + tile
    x = (tile % 2) * 2 + chip // ZS
    y = tile // 2

    def plane_peer(step, rise=0):
        other_x = (x + step[0]) % 4
        other_y = (y + step[1]) % 4
        other_tile = other_y * 2 + other_x // 2
        return other_tile, (core, (other_x % 2) * ZS + (z + rise) % ZS, other_tile)

    def column_peer(rise):
        return (core, chip - z + (z + rise) % ZS, tile)

    partner = (1 - core, chip, tile)

    barrier = pltpu.get_barrier_semaphore()
    for step in PLANE_STEPS:
        pl.semaphore_signal(barrier, inc=1, device_id=plane_peer(step)[1], device_id_type=MESH)
    for rise in COLUMN:
        pl.semaphore_signal(barrier, inc=1, device_id=column_peer(rise), device_id_type=MESH)
    pl.semaphore_signal(barrier, inc=1, device_id=partner, device_id_type=MESH)

    filter_rows(sino_copy, sino_ref, width_ref, padded, smooth, filtered)
    window_copy.wait()

    lower = iota((8, LANES), 0) < 4
    first_angle = (core * XS * ZS + chip) * 2
    for other in range(TILES):
        first = window_ref[other, first_angle]
        second = window_ref[other, first_angle + 1]
        for block in range(KEEP):
            column[z, other, block] = jnp.where(
                lower, filtered[first + block], filtered[second + block]
            ).astype(BF16)

    pl.semaphore_wait(barrier, len(PLANE_STEPS) + len(COLUMN) + 1)

    def column_copy(rise):
        return pltpu.make_async_remote_copy(
            src_ref=column.at[z],
            dst_ref=column.at[z],
            send_sem=column_send.at[rise % ZS],
            recv_sem=column_recv.at[rise % ZS],
            device_id=column_peer(rise),
            device_id_type=MESH,
        )

    def slot(shift):
        return (z + ZS - shift) % ZS

    def own_copy(shift):
        return pltpu.make_async_copy(
            column.at[slot(shift), tile], held.at[slot(shift), spot], local_sem.at[shift]
        )

    def spread(shift, rise):
        source = slot(shift)
        arrival = (shift + rise) % ZS
        steps = PLANE_STEPS
        if rise:
            steps = steps + [(0, 0)]
        else:
            own_copy(shift).start()
        for step in steps:
            other_tile, device = plane_peer(step, rise)
            pltpu.make_async_remote_copy(
                src_ref=column.at[source, other_tile],
                dst_ref=held.at[source, spot],
                send_sem=plane_send.at[arrival],
                recv_sem=plane_recv.at[arrival],
                device_id=device,
                device_id_type=MESH,
            ).start()

    def all_of_plane(shift, sem, count):
        some = held.at[slot(shift), pl.ds(0, count)]
        return pltpu.make_async_copy(some, some, sem.at[shift])

    def arrive(shift):
        if shift in (3, 4, 5):
            all_of_plane(shift, plane_recv, XS * TILES).wait()
        else:
            own_copy(shift).wait()
            all_of_plane(shift, plane_recv, XS * TILES - 1).wait()

    for rise in COLUMN:
        column_copy(rise).start()
    spread(0, 0)

    lane_f = iota((8, LANES), 1).astype(F32)
    lane16 = iota((16, LANES), 1).astype(jnp.int16)
    last_lane = lane16 == jnp.int16(LANES - 1)
    own_row = ((core * XS * ZS + chip) * ROWS_DEV).astype(F32) - (TROWS - 1) / 2.0
    partner_row = (((1 - core) * XS * ZS + chip) * ROWS_DEV).astype(F32) - (TROWS - 1) / 2.0

    @pl.loop(0, XS * ZS)
    def _(which):
        angle = (core * XS * ZS + which) * 2
        theta = jnp.where(lower, angle, angle + 1).astype(F32) * (math.pi / ANGLES)
        cosine, sine = jnp.cos(theta), jnp.sin(theta)
        spans, starts = [], []
        for half in (0, 1):
            left_end = half * LANES - (TCOLS - 1) / 2.0
            spans.append((lane_f + left_end) * cosine + float(CENTRE))
            end = jnp.where(cosine >= 0.0, left_end, left_end + LANES - 1.0)
            starts.append(end * cosine + float(CENTRE))
        for row in range(2 * ROWS_DEV):
            y = (partner_row if row < ROWS_DEV else own_row) + float(row % ROWS_DEV)
            lift = sine * y
            for half in (0, 1):
                unit = row * 2 + half
                u = spans[half] + lift
                k = u.astype(jnp.int32)
                fraction_table[which, unit] = u - k.astype(F32)
                index_table[which, unit] = k & (LANES - 1)
                start_table[which, unit] = (starts[half] + lift).astype(jnp.int32)

    def compute(source, part, units):
        which = part * ZS + source
        values, slopes = [], []
        for pair in range(TILES // 2):
            first = part * TILES + 2 * pair
            here = [
                jnp.concatenate(
                    [
                        held[source, first, block].astype(F32),
                        held[source, first + 1, block].astype(F32),
                    ],
                    axis=0,
                ).astype(BF16)
                for block in range(KEEP)
            ]
            moved = [pltpu.roll(v, LANES - 1, 1) for v in here]
            values.append(here)
            slopes.append(
                [
                    jnp.where(last_lane, moved[min(block + 1, KEEP - 1)], moved[block])
                    - here[block]
                    for block in range(KEEP)
                ]
            )
        for unit in units:
            index = index_table[which, unit]
            index = jnp.concatenate([index, index], axis=0).astype(jnp.int16)
            begin = start_table[which, unit]
            begin = jnp.concatenate([begin, begin], axis=0).astype(jnp.int16)
            part_way = fraction_table[which, unit]
            past0 = begin > lane16
            past1 = begin > lane16 + jnp.int16(LANES)
            for pair in range(TILES // 2):
                v = values[pair]
                d = slopes[pair]
                v = jnp.where(past1, v[2], jnp.where(past0, v[1], v[0]))
                d = jnp.where(past1, d[2], jnp.where(past0, d[1], d[0]))
                v = lane_gather(v, index).astype(F32)
                d = lane_gather(d, index).astype(F32)
                for half_row in (0, 1):
                    rows = slice(half_row * 8, half_row * 8 + 8)
                    at = slice(pair * 16 + half_row * 8, pair * 16 + half_row * 8 + 8)
                    term = v[rows] + part_way * d[rows]
                    total[unit, at] += term

    for rise in COLUMN[:2]:
        column_copy(rise).wait_recv()
        spread(rise % ZS, 0)
    arrive(0)
    column_copy(2).wait_recv()

    @pl.when(core == 0)
    def _():
        spread(2, 2)

    spread(2, 1)
    column_copy(-2).wait_recv()

    @pl.when(core == 1)
    def _():
        spread(ZS - 2, -2)

    spread(ZS - 2, -1)
    spread(2, 0)
    spread(ZS - 2, 0)

    def fold(unit):
        result = []
        for group in range(4):
            pieces = []
            for half in (0, 1):
                v = total[unit, group * 16 + half * 8 : group * 16 + half * 8 + 8]
                pieces.append(v + pltpu.roll(v, 4, 0))
            result.append(jnp.where(lower, pieces[0], pieces[1]))
        return jnp.concatenate(result, axis=0)

    def run(source, units):
        for part in range(XS):
            compute(source, part, units)

    @pl.loop(0, 32)
    def _(unit):
        total[unit] = jnp.zeros((64, LANES), F32)

    theirs, ours = range(16), range(16, 32)
    for shift in ORDER[:-1]:
        if shift:
            arrive(shift)
        run(slot(shift), range(32))

    arrive(ORDER[-1])
    run(slot(ORDER[-1]), theirs)
    for unit in theirs:
        partner_part[0, :, unit * LANES : (unit + 1) * LANES] = fold(unit)
    swap = pltpu.make_async_remote_copy(
        src_ref=partner_part,
        dst_ref=arrived_part,
        send_sem=part_send,
        recv_sem=part_recv,
        device_id=partner,
        device_id_type=MESH,
    )
    swap.start()
    run(slot(ORDER[-1]), ours)
    for unit in ours:
        out_ref[0, :, (unit - 16) * LANES : (unit - 15) * LANES] = fold(unit)
    swap.wait()
    for rise in COLUMN:
        column_copy(rise).wait_send()
    for shift in range(ZS):
        all_of_plane(shift, plane_send, XS * TILES - (shift not in (3, 4, 5))).wait()


def body(sinogram, paganin_width, window_block):
    smem = pl.BlockSpec(memory_space=pltpu.SMEM)
    hbm = pl.BlockSpec(memory_space=pltpu.HBM)
    vmem = pl.BlockSpec(memory_space=pltpu.VMEM)
    part = jax.ShapeDtypeStruct((1, 32, ROWS_DEV * TCOLS), F32)
    own, arrived = pl.pallas_call(
        kernel,
        out_shape=(part, part),
        in_specs=[hbm, smem, hbm],
        out_specs=(vmem, vmem),
        scratch_shapes=[
            pltpu.VMEM((2, 4, BLOCKS * LANES), F32),
            pltpu.SMEM((TILES, ANGLES), jnp.int32),
            pltpu.VMEM((272, LANES), F32),
            pltpu.VMEM((272, LANES), F32),
            pltpu.VMEM((BLOCKS - 1, 8, LANES), F32),
            pltpu.VMEM((ZS, TILES, KEEP, 8, LANES), BF16),
            pltpu.VMEM((ZS, XS * TILES, KEEP, 8, LANES), BF16),
            pltpu.VMEM((32, 64, LANES), F32),
            pltpu.VMEM((1, 32, ROWS_DEV * TCOLS), F32),
            pltpu.VMEM((XS * ZS, 32, 8, LANES), jnp.int32),
            pltpu.VMEM((XS * ZS, 32, 8, LANES), jnp.int32),
            pltpu.VMEM((XS * ZS, 32, 8, LANES), F32),
            pltpu.SemaphoreType.DMA((2,)),
            pltpu.SemaphoreType.DMA((ZS,)),
            pltpu.SemaphoreType.DMA((ZS,)),
            pltpu.SemaphoreType.DMA((ZS,)),
            pltpu.SemaphoreType.DMA((ZS,)),
            pltpu.SemaphoreType.DMA((ZS,)),
            pltpu.SemaphoreType.DMA,
            pltpu.SemaphoreType.DMA,
        ],
        compiler_params=pltpu.CompilerParams(
            collective_id=0, has_side_effects=True, vmem_limit_bytes=32 << 20
        ),
    )(
        pltpu.with_memory_space_constraint(sinogram, pltpu.HBM),
        paganin_width,
        pltpu.with_memory_space_constraint(window_block.T, pltpu.HBM),
    )
    return own + arrived


def solution(mesh):
    in_specs = (P(("segment", "angle"), "tile", None), P(), P())
    out_specs = P("tile", None, ("segment", "angle"))
    return jax.shard_map(body, mesh=mesh, in_specs=in_specs, out_specs=out_specs, check_vma=False)
```

```python
import functools
import math

import jax
import jax.numpy as jnp
from jax import lax
from jax.experimental import pallas as pl
from jax.experimental.pallas import tpu as pltpu
from jax.sharding import PartitionSpec as P

MESH = pl.DeviceIdType.MESH
LANES = 128
BAND = 128
ROWS_DEV = 8
TCOLS = 256
ANGLES = 64
TROWS = 256
TILES = 8
ZS = 8
XS = 2
BLOCKS = 32
KEEP = 3
BINS_SHIFT = 64
CENTRE = 256 - BINS_SHIFT
COLUMN = (1, -1, 2, -2)
LATE = 3
ORDER = (1, 7, 3, 5, 2, 6, 4)


def ring_distance(step):
    return sum(min(part, 4 - part) for part in step)


PLANE_STEPS = sorted(
    ((a, b) for a in range(4) for b in range(4) if a or b), key=ring_distance, reverse=True
)

F32 = jnp.float32
BF16 = jnp.bfloat16

GATHER = lax.GatherDimensionNumbers(
    offset_dims=(),
    collapsed_slice_dims=(1,),
    start_index_map=(1,),
    operand_batching_dims=(0,),
    start_indices_batching_dims=(0,),
)


def lane_gather(values, index):
    return lax.gather(
        values, index[:, :, None], GATHER, (1, 1), mode=lax.GatherScatterMode.PROMISE_IN_BOUNDS
    )


def iota(shape, axis):
    return lax.broadcasted_iota(jnp.int32, shape, axis)


def split(value):
    high = value.astype(BF16)
    return high, (value - high.astype(F32)).astype(BF16)


def dot3(left, right):
    left_high, left_low = split(left)
    right_high, right_low = split(right)
    return (
        jnp.dot(left_high, right_high, preferred_element_type=F32)
        + jnp.dot(left_low, right_high, preferred_element_type=F32)
        + jnp.dot(left_high, right_low, preferred_element_type=F32)
    )


def smoothing_band(width):
    shape = (3 * LANES, LANES)
    offset = iota(shape, 0) - LANES - iota(shape, 1)
    spread = jnp.abs(offset).astype(F32)
    taps = jnp.exp(-(iota((1, LANES), 1) + 1).astype(F32) / width)
    total = 1.0 + 2.0 * jnp.sum(taps)
    return jnp.where(jnp.abs(offset) <= BAND, jnp.exp(-spread / width) / total, 0.0)


def ramp_band():
    shape = (4 * LANES, LANES)
    offset = iota(shape, 0) - LANES - BINS_SHIFT - iota(shape, 1)
    size = jnp.abs(offset)
    spread = size.astype(F32)
    odd = jnp.where(
        (size <= BAND) & (size % 2 == 1),
        -1.0 / (math.pi * math.pi * jnp.maximum(spread * spread, 1.0)),
        0.0,
    )
    return jnp.where(offset == 0, 0.25, odd)


def filter_rows(sino_copy, sino_ref, width_ref, padded, smooth, filtered):
    smoothing = smoothing_band(jnp.full((1, 1), width_ref[0], F32))
    ramp = ramp_band()
    zero = jnp.zeros((8, LANES), F32)
    padded[0:8] = zero
    padded[264:272] = zero
    smooth[0:8] = zero
    smooth[264:272] = zero
    sino_copy.wait()
    for block in range(BLOCKS):
        columns = slice(block * LANES, (block + 1) * LANES)
        padded[(block + 1) * 8 : (block + 2) * 8] = jnp.concatenate(
            [sino_ref[0, :, columns], sino_ref[1, :, columns]], axis=0
        )
    left = jnp.concatenate([padded[8 * k : 8 * k + 256] for k in range(3)], axis=1)
    smooth[8:264] = dot3(left, smoothing)
    left = jnp.concatenate([smooth[8 * k : 8 * k + 248] for k in range(4)], axis=1)
    filtered[...] = dot3(left, ramp).reshape(BLOCKS - 1, 8, LANES)


def kernel(
    sino_hbm,
    width_ref,
    window_hbm,
    out_ref,
    arrived_part,
    sino_ref,
    window_ref,
    padded,
    smooth,
    filtered,
    column,
    held,
    total,
    partner_part,
    index_table,
    start_table,
    fraction_table,
    input_sem,
    column_send,
    column_recv,
    plane_send,
    plane_recv,
    local_sem,
    part_send,
    part_recv,
):
    sino_copy = pltpu.make_async_copy(sino_hbm, sino_ref, input_sem.at[0])
    window_copy = pltpu.make_async_copy(window_hbm, window_ref, input_sem.at[1])
    sino_copy.start()
    window_copy.start()
    core = lax.axis_index("segment")
    chip = lax.axis_index("angle")
    tile = lax.axis_index("tile")
    z = chip % ZS
    spot = (chip // ZS) * TILES + tile
    x = (tile % 2) * 2 + chip // ZS
    y = tile // 2

    def plane_peer(step, rise=0):
        other_x = (x + step[0]) % 4
        other_y = (y + step[1]) % 4
        other_tile = other_y * 2 + other_x // 2
        return other_tile, (core, (other_x % 2) * ZS + (z + rise) % ZS, other_tile)

    def column_peer(rise):
        return (core, chip - z + (z + rise) % ZS, tile)

    partner = (1 - core, chip, tile)

    barrier = pltpu.get_barrier_semaphore()
    for step in PLANE_STEPS:
        pl.semaphore_signal(barrier, inc=1, device_id=plane_peer(step)[1], device_id_type=MESH)
    for rise in COLUMN:
        pl.semaphore_signal(barrier, inc=1, device_id=column_peer(rise), device_id_type=MESH)
    pl.semaphore_signal(barrier, inc=1, device_id=partner, device_id_type=MESH)

    filter_rows(sino_copy, sino_ref, width_ref, padded, smooth, filtered)
    window_copy.wait()

    lower = iota((8, LANES), 0) < 4
    first_angle = (core * XS * ZS + chip) * 2
    for other in range(TILES):
        first = window_ref[other, first_angle]
        second = window_ref[other, first_angle + 1]
        for block in range(KEEP):
            column[z, other, block] = jnp.where(
                lower, filtered[first + block], filtered[second + block]
            ).astype(BF16)

    pl.semaphore_wait(barrier, len(PLANE_STEPS) + len(COLUMN) + 1)

    def column_copy(rise):
        return pltpu.make_async_remote_copy(
            src_ref=column.at[z],
            dst_ref=column.at[z],
            send_sem=column_send.at[rise % ZS],
            recv_sem=column_recv.at[rise % ZS],
            device_id=column_peer(rise),
            device_id_type=MESH,
        )

    def slot(shift):
        return (z + ZS - shift) % ZS

    def own_copy(shift):
        return pltpu.make_async_copy(
            column.at[slot(shift), tile], held.at[slot(shift), spot], local_sem.at[shift]
        )

    def spread(shift, rise):
        source = slot(shift)
        arrival = (shift + rise) % ZS
        steps = PLANE_STEPS
        if rise:
            steps = steps + [(0, 0)]
        else:
            own_copy(shift).start()
        for step in steps:
            other_tile, device = plane_peer(step, rise)
            pltpu.make_async_remote_copy(
                src_ref=column.at[source, other_tile],
                dst_ref=held.at[source, spot],
                send_sem=plane_send.at[arrival],
                recv_sem=plane_recv.at[arrival],
                device_id=device,
                device_id_type=MESH,
            ).start()

    def all_of_plane(shift, sem, count):
        some = held.at[slot(shift), pl.ds(0, count)]
        return pltpu.make_async_copy(some, some, sem.at[shift])

    def arrive(shift):
        if shift in (3, 4, 5):
            all_of_plane(shift, plane_recv, XS * TILES).wait()
        else:
            own_copy(shift).wait()
            all_of_plane(shift, plane_recv, XS * TILES - 1).wait()

    for rise in COLUMN:
        column_copy(rise).start()
    spread(0, 0)

    lane_f = iota((8, LANES), 1).astype(F32)
    lane16 = iota((16, LANES), 1).astype(jnp.int16)
    last_lane = lane16 == jnp.int16(LANES - 1)
    own_row = ((core * XS * ZS + chip) * ROWS_DEV).astype(F32) - (TROWS - 1) / 2.0
    partner_row = (((1 - core) * XS * ZS + chip) * ROWS_DEV).astype(F32) - (TROWS - 1) / 2.0

    @pl.loop(0, XS * ZS)
    def _(which):
        angle = (core * XS * ZS + which) * 2
        theta = jnp.where(lower, angle, angle + 1).astype(F32) * (math.pi / ANGLES)
        cosine, sine = jnp.cos(theta), jnp.sin(theta)
        spans, starts = [], []
        for half in (0, 1):
            left_end = half * LANES - (TCOLS - 1) / 2.0
            spans.append((lane_f + left_end) * cosine + float(CENTRE))
            end = jnp.where(cosine >= 0.0, left_end, left_end + LANES - 1.0)
            starts.append(end * cosine + float(CENTRE))
        for row in range(2 * ROWS_DEV):
            y = (partner_row if row < ROWS_DEV else own_row) + float(row % ROWS_DEV)
            lift = sine * y
            for half in (0, 1):
                unit = row * 2 + half
                u = spans[half] + lift
                k = u.astype(jnp.int32)
                fraction_table[which, unit] = u - k.astype(F32)
                index_table[which, unit] = k & (LANES - 1)
                start_table[which, unit] = (starts[half] + lift).astype(jnp.int32)

    def compute(source, part, units):
        which = part * ZS + source
        values, slopes = [], []
        for pair in range(TILES // 2):
            first = part * TILES + 2 * pair
            here = [
                jnp.concatenate(
                    [
                        held[source, first, block].astype(F32),
                        held[source, first + 1, block].astype(F32),
                    ],
                    axis=0,
                ).astype(BF16)
                for block in range(KEEP)
            ]
            moved = [pltpu.roll(v, LANES - 1, 1) for v in here]
            values.append(here)
            slopes.append(
                [
                    jnp.where(last_lane, moved[min(block + 1, KEEP - 1)], moved[block])
                    - here[block]
                    for block in range(KEEP)
                ]
            )
        for unit in units:
            index = index_table[which, unit]
            index = jnp.concatenate([index, index], axis=0).astype(jnp.int16)
            begin = start_table[which, unit]
            begin = jnp.concatenate([begin, begin], axis=0).astype(jnp.int16)
            part_way = fraction_table[which, unit]
            past0 = begin > lane16
            past1 = begin > lane16 + jnp.int16(LANES)
            for pair in range(TILES // 2):
                v = values[pair]
                d = slopes[pair]
                v = jnp.where(past1, v[2], jnp.where(past0, v[1], v[0]))
                d = jnp.where(past1, d[2], jnp.where(past0, d[1], d[0]))
                v = lane_gather(v, index).astype(F32)
                d = lane_gather(d, index).astype(F32)
                for half_row in (0, 1):
                    rows = slice(half_row * 8, half_row * 8 + 8)
                    at = slice(pair * 16 + half_row * 8, pair * 16 + half_row * 8 + 8)
                    term = v[rows] + part_way * d[rows]
                    total[unit, at] += term

    for rise in COLUMN[:2]:
        column_copy(rise).wait_recv()
        spread(rise % ZS, 0)
    def fold(unit):
        result = []
        for group in range(4):
            pieces = []
            for half in (0, 1):
                v = total[unit, group * 16 + half * 8 : group * 16 + half * 8 + 8]
                pieces.append(v + pltpu.roll(v, 4, 0))
            result.append(jnp.where(lower, pieces[0], pieces[1]))
        return jnp.concatenate(result, axis=0)

    def run(source, units):
        for part in range(XS):
            compute(source, part, units)

    @pl.loop(0, 32)
    def _(unit):
        total[unit] = jnp.zeros((64, LANES), F32)

    arrive(0)
    spread(1, 2)
    spread(ZS - 1, -2)
    run(slot(0), range(32))

    column_copy(2).wait_recv()
    column_copy(-2).wait_recv()
    spread(2, 0)
    spread(ZS - 2, 0)

    @pl.when(core == 0)
    def _():
        spread(2, 2)

    @pl.when(core == 1)
    def _():
        spread(ZS - 2, -2)

    theirs, ours = range(16), range(16, 32)
    for shift in ORDER[:-LATE]:
        arrive(shift)
        run(slot(shift), range(32))

    for shift in ORDER[-LATE:]:
        arrive(shift)
        run(slot(shift), theirs)
    for unit in theirs:
        partner_part[0, :, unit * LANES : (unit + 1) * LANES] = fold(unit)
    swap = pltpu.make_async_remote_copy(
        src_ref=partner_part,
        dst_ref=arrived_part,
        send_sem=part_send,
        recv_sem=part_recv,
        device_id=partner,
        device_id_type=MESH,
    )
    swap.start()
    for shift in ORDER[-LATE:]:
        run(slot(shift), ours)
    for unit in ours:
        out_ref[0, :, (unit - 16) * LANES : (unit - 15) * LANES] = fold(unit)
    swap.wait()
    for rise in COLUMN:
        column_copy(rise).wait_send()
    for shift in range(ZS):
        all_of_plane(shift, plane_send, XS * TILES - (shift not in (3, 4, 5))).wait()


def body(sinogram, paganin_width, window_block):
    smem = pl.BlockSpec(memory_space=pltpu.SMEM)
    hbm = pl.BlockSpec(memory_space=pltpu.HBM)
    vmem = pl.BlockSpec(memory_space=pltpu.VMEM)
    part = jax.ShapeDtypeStruct((1, 32, ROWS_DEV * TCOLS), F32)
    own, arrived = pl.pallas_call(
        kernel,
        out_shape=(part, part),
        in_specs=[hbm, smem, hbm],
        out_specs=(vmem, vmem),
        scratch_shapes=[
            pltpu.VMEM((2, 4, BLOCKS * LANES), F32),
            pltpu.SMEM((TILES, ANGLES), jnp.int32),
            pltpu.VMEM((272, LANES), F32),
            pltpu.VMEM((272, LANES), F32),
            pltpu.VMEM((BLOCKS - 1, 8, LANES), F32),
            pltpu.VMEM((ZS, TILES, KEEP, 8, LANES), BF16),
            pltpu.VMEM((ZS, XS * TILES, KEEP, 8, LANES), BF16),
            pltpu.VMEM((32, 64, LANES), F32),
            pltpu.VMEM((1, 32, ROWS_DEV * TCOLS), F32),
            pltpu.VMEM((XS * ZS, 32, 8, LANES), jnp.int32),
            pltpu.VMEM((XS * ZS, 32, 8, LANES), jnp.int32),
            pltpu.VMEM((XS * ZS, 32, 8, LANES), F32),
            pltpu.SemaphoreType.DMA((2,)),
            pltpu.SemaphoreType.DMA((ZS,)),
            pltpu.SemaphoreType.DMA((ZS,)),
            pltpu.SemaphoreType.DMA((ZS,)),
            pltpu.SemaphoreType.DMA((ZS,)),
            pltpu.SemaphoreType.DMA((ZS,)),
            pltpu.SemaphoreType.DMA,
            pltpu.SemaphoreType.DMA,
        ],
        compiler_params=pltpu.CompilerParams(
            collective_id=0, has_side_effects=True, vmem_limit_bytes=32 << 20
        ),
    )(
        pltpu.with_memory_space_constraint(sinogram, pltpu.HBM),
        paganin_width,
        pltpu.with_memory_space_constraint(window_block.T, pltpu.HBM),
    )
    return own + arrived


def solution(mesh):
    in_specs = (P(("segment", "angle"), "tile", None), P(), P())
    out_specs = P("tile", None, ("segment", "angle"))
    return jax.shard_map(body, mesh=mesh, in_specs=in_specs, out_specs=out_specs, check_vma=False)
```

```python
import functools
import math

import jax
import jax.numpy as jnp
from jax import lax
from jax.experimental import pallas as pl
from jax.experimental.pallas import tpu as pltpu
from jax.sharding import PartitionSpec as P

MESH = pl.DeviceIdType.MESH
LANES = 128
BAND = 128
ROWS_DEV = 8
TCOLS = 256
ANGLES = 64
TROWS = 256
TILES = 8
ZS = 8
XS = 2
BLOCKS = 32
KEEP = 3
BINS_SHIFT = 64
CENTRE = 256 - BINS_SHIFT
COLUMN = (1, -1, 2, -2)
LATE = 5
ORDER = (1, 7, 3, 5, 2, 6, 4)


def ring_distance(step):
    return sum(min(part, 4 - part) for part in step)


PLANE_STEPS = sorted(
    ((a, b) for a in range(4) for b in range(4) if a or b), key=ring_distance, reverse=True
)

F32 = jnp.float32
BF16 = jnp.bfloat16

GATHER = lax.GatherDimensionNumbers(
    offset_dims=(),
    collapsed_slice_dims=(1,),
    start_index_map=(1,),
    operand_batching_dims=(0,),
    start_indices_batching_dims=(0,),
)


def lane_gather(values, index):
    return lax.gather(
        values, index[:, :, None], GATHER, (1, 1), mode=lax.GatherScatterMode.PROMISE_IN_BOUNDS
    )


def iota(shape, axis):
    return lax.broadcasted_iota(jnp.int32, shape, axis)


def split(value):
    high = value.astype(BF16)
    return high, (value - high.astype(F32)).astype(BF16)


def dot3(left, right):
    left_high, left_low = split(left)
    right_high, right_low = split(right)
    return (
        jnp.dot(left_high, right_high, preferred_element_type=F32)
        + jnp.dot(left_low, right_high, preferred_element_type=F32)
        + jnp.dot(left_high, right_low, preferred_element_type=F32)
    )


def smoothing_band(width):
    shape = (3 * LANES, LANES)
    offset = iota(shape, 0) - LANES - iota(shape, 1)
    spread = jnp.abs(offset).astype(F32)
    taps = jnp.exp(-(iota((1, LANES), 1) + 1).astype(F32) / width)
    total = 1.0 + 2.0 * jnp.sum(taps)
    return jnp.where(jnp.abs(offset) <= BAND, jnp.exp(-spread / width) / total, 0.0)


def ramp_band():
    shape = (4 * LANES, LANES)
    offset = iota(shape, 0) - LANES - BINS_SHIFT - iota(shape, 1)
    size = jnp.abs(offset)
    spread = size.astype(F32)
    odd = jnp.where(
        (size <= BAND) & (size % 2 == 1),
        -1.0 / (math.pi * math.pi * jnp.maximum(spread * spread, 1.0)),
        0.0,
    )
    return jnp.where(offset == 0, 0.25, odd)


def filter_rows(sino_copy, sino_ref, width_ref, padded, smooth, filtered):
    smoothing = smoothing_band(jnp.full((1, 1), width_ref[0], F32))
    ramp = ramp_band()
    zero = jnp.zeros((8, LANES), F32)
    padded[0:8] = zero
    padded[264:272] = zero
    smooth[0:8] = zero
    smooth[264:272] = zero
    sino_copy.wait()
    for block in range(BLOCKS):
        columns = slice(block * LANES, (block + 1) * LANES)
        padded[(block + 1) * 8 : (block + 2) * 8] = jnp.concatenate(
            [sino_ref[0, :, columns], sino_ref[1, :, columns]], axis=0
        )
    left = jnp.concatenate([padded[8 * k : 8 * k + 256] for k in range(3)], axis=1)
    smooth[8:264] = dot3(left, smoothing)
    left = jnp.concatenate([smooth[8 * k : 8 * k + 248] for k in range(4)], axis=1)
    filtered[...] = dot3(left, ramp).reshape(BLOCKS - 1, 8, LANES)


def kernel(
    sino_hbm,
    width_ref,
    window_hbm,
    out_ref,
    arrived_part,
    sino_ref,
    window_ref,
    padded,
    smooth,
    filtered,
    column,
    held,
    total,
    partner_part,
    index_table,
    start_table,
    fraction_table,
    input_sem,
    column_send,
    column_recv,
    plane_send,
    plane_recv,
    local_sem,
    part_send,
    part_recv,
):
    sino_copy = pltpu.make_async_copy(sino_hbm, sino_ref, input_sem.at[0])
    window_copy = pltpu.make_async_copy(window_hbm, window_ref, input_sem.at[1])
    sino_copy.start()
    window_copy.start()
    core = lax.axis_index("segment")
    chip = lax.axis_index("angle")
    tile = lax.axis_index("tile")
    z = chip % ZS
    spot = (chip // ZS) * TILES + tile
    x = (tile % 2) * 2 + chip // ZS
    y = tile // 2

    def plane_peer(step, rise=0):
        other_x = (x + step[0]) % 4
        other_y = (y + step[1]) % 4
        other_tile = other_y * 2 + other_x // 2
        return other_tile, (core, (other_x % 2) * ZS + (z + rise) % ZS, other_tile)

    def column_peer(rise):
        return (core, chip - z + (z + rise) % ZS, tile)

    partner = (1 - core, chip, tile)

    barrier = pltpu.get_barrier_semaphore()
    for step in PLANE_STEPS:
        pl.semaphore_signal(barrier, inc=1, device_id=plane_peer(step)[1], device_id_type=MESH)
    for rise in COLUMN:
        pl.semaphore_signal(barrier, inc=1, device_id=column_peer(rise), device_id_type=MESH)
    pl.semaphore_signal(barrier, inc=1, device_id=partner, device_id_type=MESH)

    filter_rows(sino_copy, sino_ref, width_ref, padded, smooth, filtered)
    window_copy.wait()

    lower = iota((8, LANES), 0) < 4
    first_angle = (core * XS * ZS + chip) * 2
    for other in range(TILES):
        first = window_ref[other, first_angle]
        second = window_ref[other, first_angle + 1]
        for block in range(KEEP):
            column[z, other, block] = jnp.where(
                lower, filtered[first + block], filtered[second + block]
            ).astype(BF16)

    pl.semaphore_wait(barrier, len(PLANE_STEPS) + len(COLUMN) + 1)

    def column_copy(rise):
        return pltpu.make_async_remote_copy(
            src_ref=column.at[z],
            dst_ref=column.at[z],
            send_sem=column_send.at[rise % ZS],
            recv_sem=column_recv.at[rise % ZS],
            device_id=column_peer(rise),
            device_id_type=MESH,
        )

    def slot(shift):
        return (z + ZS - shift) % ZS

    def own_copy(shift):
        return pltpu.make_async_copy(
            column.at[slot(shift), tile], held.at[slot(shift), spot], local_sem.at[shift]
        )

    def spread(shift, rise):
        source = slot(shift)
        arrival = (shift + rise) % ZS
        steps = PLANE_STEPS
        if rise:
            steps = steps + [(0, 0)]
        else:
            own_copy(shift).start()
        for step in steps:
            other_tile, device = plane_peer(step, rise)
            pltpu.make_async_remote_copy(
                src_ref=column.at[source, other_tile],
                dst_ref=held.at[source, spot],
                send_sem=plane_send.at[arrival],
                recv_sem=plane_recv.at[arrival],
                device_id=device,
                device_id_type=MESH,
            ).start()

    def all_of_plane(shift, sem, count):
        some = held.at[slot(shift), pl.ds(0, count)]
        return pltpu.make_async_copy(some, some, sem.at[shift])

    def arrive(shift):
        if shift in (3, 4, 5):
            all_of_plane(shift, plane_recv, XS * TILES).wait()
        else:
            own_copy(shift).wait()
            all_of_plane(shift, plane_recv, XS * TILES - 1).wait()

    for rise in COLUMN:
        column_copy(rise).start()
    spread(0, 0)

    lane_f = iota((8, LANES), 1).astype(F32)
    lane16 = iota((16, LANES), 1).astype(jnp.int16)
    last_lane = lane16 == jnp.int16(LANES - 1)
    own_row = ((core * XS * ZS + chip) * ROWS_DEV).astype(F32) - (TROWS - 1) / 2.0
    partner_row = (((1 - core) * XS * ZS + chip) * ROWS_DEV).astype(F32) - (TROWS - 1) / 2.0

    @pl.loop(0, XS * ZS)
    def _(which):
        angle = (core * XS * ZS + which) * 2
        theta = jnp.where(lower, angle, angle + 1).astype(F32) * (math.pi / ANGLES)
        cosine, sine = jnp.cos(theta), jnp.sin(theta)
        spans, starts = [], []
        for half in (0, 1):
            left_end = half * LANES - (TCOLS - 1) / 2.0
            spans.append((lane_f + left_end) * cosine + float(CENTRE))
            end = jnp.where(cosine >= 0.0, left_end, left_end + LANES - 1.0)
            starts.append(end * cosine + float(CENTRE))
        for row in range(2 * ROWS_DEV):
            y = (partner_row if row < ROWS_DEV else own_row) + float(row % ROWS_DEV)
            lift = sine * y
            for half in (0, 1):
                unit = row * 2 + half
                u = spans[half] + lift
                k = u.astype(jnp.int32)
                fraction_table[which, unit] = u - k.astype(F32)
                index_table[which, unit] = k & (LANES - 1)
                start_table[which, unit] = (starts[half] + lift).astype(jnp.int32)

    def compute(source, part, units):
        which = part * ZS + source
        values, slopes = [], []
        for pair in range(TILES // 2):
            first = part * TILES + 2 * pair
            here = [
                jnp.concatenate(
                    [
                        held[source, first, block].astype(F32),
                        held[source, first + 1, block].astype(F32),
                    ],
                    axis=0,
                ).astype(BF16)
                for block in range(KEEP)
            ]
            moved = [pltpu.roll(v, LANES - 1, 1) for v in here]
            values.append(here)
            slopes.append(
                [
                    jnp.where(last_lane, moved[min(block + 1, KEEP - 1)], moved[block])
                    - here[block]
                    for block in range(KEEP)
                ]
            )
        for unit in units:
            index = index_table[which, unit]
            index = jnp.concatenate([index, index], axis=0).astype(jnp.int16)
            begin = start_table[which, unit]
            begin = jnp.concatenate([begin, begin], axis=0).astype(jnp.int16)
            part_way = fraction_table[which, unit]
            past0 = begin > lane16
            past1 = begin > lane16 + jnp.int16(LANES)
            for pair in range(TILES // 2):
                v = values[pair]
                d = slopes[pair]
                v = jnp.where(past1, v[2], jnp.where(past0, v[1], v[0]))
                d = jnp.where(past1, d[2], jnp.where(past0, d[1], d[0]))
                v = lane_gather(v, index).astype(F32)
                d = lane_gather(d, index).astype(F32)
                for half_row in (0, 1):
                    rows = slice(half_row * 8, half_row * 8 + 8)
                    at = slice(pair * 16 + half_row * 8, pair * 16 + half_row * 8 + 8)
                    term = v[rows] + part_way * d[rows]
                    total[unit, at] += term

    for rise in COLUMN[:2]:
        column_copy(rise).wait_recv()
        spread(rise % ZS, 0)
    def fold(unit):
        result = []
        for group in range(4):
            pieces = []
            for half in (0, 1):
                v = total[unit, group * 16 + half * 8 : group * 16 + half * 8 + 8]
                pieces.append(v + pltpu.roll(v, 4, 0))
            result.append(jnp.where(lower, pieces[0], pieces[1]))
        return jnp.concatenate(result, axis=0)

    def run(source, units):
        for part in range(XS):
            compute(source, part, units)

    @pl.loop(0, 32)
    def _(unit):
        total[unit] = jnp.zeros((64, LANES), F32)

    arrive(0)
    spread(1, 2)
    spread(ZS - 1, -2)
    run(slot(0), range(32))

    column_copy(2).wait_recv()
    column_copy(-2).wait_recv()
    spread(2, 0)
    spread(ZS - 2, 0)

    @pl.when(core == 0)
    def _():
        spread(2, 2)

    @pl.when(core == 1)
    def _():
        spread(ZS - 2, -2)

    theirs, ours = range(16), range(16, 32)
    for shift in ORDER[:-LATE]:
        arrive(shift)
        run(slot(shift), range(32))

    for shift in ORDER[-LATE:]:
        arrive(shift)
        run(slot(shift), theirs)
    for unit in theirs:
        partner_part[0, :, unit * LANES : (unit + 1) * LANES] = fold(unit)
    swap = pltpu.make_async_remote_copy(
        src_ref=partner_part,
        dst_ref=arrived_part,
        send_sem=part_send,
        recv_sem=part_recv,
        device_id=partner,
        device_id_type=MESH,
    )
    swap.start()
    for shift in ORDER[-LATE:]:
        run(slot(shift), ours)
    for unit in ours:
        out_ref[0, :, (unit - 16) * LANES : (unit - 15) * LANES] = fold(unit)
    swap.wait()
    for rise in COLUMN:
        column_copy(rise).wait_send()
    for shift in range(ZS):
        all_of_plane(shift, plane_send, XS * TILES - (shift not in (3, 4, 5))).wait()


def body(sinogram, paganin_width, window_block):
    smem = pl.BlockSpec(memory_space=pltpu.SMEM)
    hbm = pl.BlockSpec(memory_space=pltpu.HBM)
    vmem = pl.BlockSpec(memory_space=pltpu.VMEM)
    part = jax.ShapeDtypeStruct((1, 32, ROWS_DEV * TCOLS), F32)
    own, arrived = pl.pallas_call(
        kernel,
        out_shape=(part, part),
        in_specs=[hbm, smem, hbm],
        out_specs=(vmem, vmem),
        scratch_shapes=[
            pltpu.VMEM((2, 4, BLOCKS * LANES), F32),
            pltpu.SMEM((TILES, ANGLES), jnp.int32),
            pltpu.VMEM((272, LANES), F32),
            pltpu.VMEM((272, LANES), F32),
            pltpu.VMEM((BLOCKS - 1, 8, LANES), F32),
            pltpu.VMEM((ZS, TILES, KEEP, 8, LANES), BF16),
            pltpu.VMEM((ZS, XS * TILES, KEEP, 8, LANES), BF16),
            pltpu.VMEM((32, 64, LANES), F32),
            pltpu.VMEM((1, 32, ROWS_DEV * TCOLS), F32),
            pltpu.VMEM((XS * ZS, 32, 8, LANES), jnp.int32),
            pltpu.VMEM((XS * ZS, 32, 8, LANES), jnp.int32),
            pltpu.VMEM((XS * ZS, 32, 8, LANES), F32),
            pltpu.SemaphoreType.DMA((2,)),
            pltpu.SemaphoreType.DMA((ZS,)),
            pltpu.SemaphoreType.DMA((ZS,)),
            pltpu.SemaphoreType.DMA((ZS,)),
            pltpu.SemaphoreType.DMA((ZS,)),
            pltpu.SemaphoreType.DMA((ZS,)),
            pltpu.SemaphoreType.DMA,
            pltpu.SemaphoreType.DMA,
        ],
        compiler_params=pltpu.CompilerParams(
            collective_id=0, has_side_effects=True, vmem_limit_bytes=32 << 20
        ),
    )(
        pltpu.with_memory_space_constraint(sinogram, pltpu.HBM),
        paganin_width,
        pltpu.with_memory_space_constraint(window_block.T, pltpu.HBM),
    )
    return own + arrived


def solution(mesh):
    in_specs = (P(("segment", "angle"), "tile", None), P(), P())
    out_specs = P("tile", None, ("segment", "angle"))
    return jax.shard_map(body, mesh=mesh, in_specs=in_specs, out_specs=out_specs, check_vma=False)
```
